32 devices in a mesh: gx: 4 (over y, x), gy: 4 (over z), gz: 2 (over core).
Axes of the slice: x: 2, y: 2, z: 4, core: 2. Of those that a mesh axis runs over, the one named last changes fastest.
Arguments:
- particles: float32 [32, 32, 16, 128], P('gx', 'gy', 'gz'), may hold values from -6 to 6, as said below
- counts: int32 [32, 32, 16], P('gx', 'gy', 'gz'), may hold values from 1 to 32, as said below
Outputs:
- potential: float32 [32, 32, 512], P('gx', 'gy', 'gz')
- near_potential: float32 [32, 32, 512], P('gx', 'gy', 'gz')
The draws below stay inside these ranges and needn't reach their ends.
Inputs may be any that keep to these rules, and one draw needn't show every extreme that they name: `particles`: in each leaf the first 96 entries are offsets from the leaf's centre in leaf sides, three blocks of 32 for the three coordinates, within -0.5 and 0.5; the last 32 are strengths. `counts`: slots from the count on are padding; some leaf is full.
All inputs are finite; a program needn't handle non-finite values.
Results may differ from the reference program's by a relative error of at most 0.0003.
Values sent between devices are 32-bit elements; how exact they have to be, the bound alone decides.
A program may use at most 64 MiB of HBM per device.

```python
import math
import jax
import jax.numpy as jnp
from jax import lax

P_SIZE = 32
Q = 64
SIDE = 8
DEPTH = 1
NX = 32
NY = 32
NZ = 16
N_GX = 4
N_GY = 4
N_GZ = 2


def draw_particles(key, part):
    first, second = jax.random.split(jax.random.fold_in(key, 11))
    offsets = jax.random.uniform(first, (NX, NY, NZ, 3 * P_SIZE), jnp.float32, -0.5, 0.5)
    strengths = jnp.clip(jax.random.normal(second, (NX, NY, NZ, P_SIZE), jnp.float32), -6.0, 6.0)
    return jnp.concatenate([offsets, strengths], axis=3)


def draw_counts(key, part):
    first, second, third = jax.random.split(jax.random.fold_in(key, 23), 3)
    values = jax.random.randint(first, (NX, NY, NZ), 1, P_SIZE + 1, dtype=jnp.int32)
    leaves_all = NX * NY * NZ
    chosen_full = jax.random.randint(second, (), 0, leaves_all, dtype=jnp.int32)
    chosen_single = jax.random.randint(third, (), 0, leaves_all, dtype=jnp.int32)
    order = jnp.arange(leaves_all, dtype=jnp.int32).reshape(NX, NY, NZ)
    values = jnp.where(order == chosen_single, 1, values)
    return jnp.where(order == chosen_full, P_SIZE, values)


def setup_inputs(seed: int = 0) -> dict:
    keys = jax.random.split(jax.random.key(seed), 3)
    return {
        "particles": draw_particles(jax.random.fold_in(keys[2], 71), 0),
        "counts": draw_counts(jax.random.fold_in(keys[2], 71), 0),
    }


INV_FOUR_PI = 0.07957747154594767
INNER = 0.9
OUTER = 1.5
PARENT_CHECK = 3.0
SOFTEN_SQUARED = 0.0625
REGULAR = 0.01
HIGHEST = lax.Precision.HIGHEST

def sphere(number):
    order = jnp.arange(number, dtype=jnp.float32)
    height = 1.0 - (2.0 * order + 1.0) / number
    radial = jnp.sqrt(1.0 - height * height)
    turning = order * (math.pi * (3.0 - math.sqrt(5.0)))
    return jnp.stack([radial * jnp.cos(turning), radial * jnp.sin(turning), height])

def green(first, second, third):
    return INV_FOUR_PI / jnp.sqrt(first * first + second * second + third * third)

def factor_lower(normal):
    number = normal.shape[0]
    rows = jnp.arange(number, dtype=jnp.int32)

    def column_turn(column, factor):
        column = column.astype(jnp.int32)
        select = (rows == column).astype(jnp.float32)
        own_row = jnp.dot(select, factor, precision=HIGHEST)
        residue = jnp.dot(normal, select, precision=HIGHEST) - jnp.dot(factor, own_row, precision=HIGHEST)
        pivot = jnp.sqrt(jnp.dot(select, residue, precision=HIGHEST))
        newcol = jnp.where(rows >= column, residue / pivot, 0.0)
        return factor + newcol[:, None] * select[None, :]
    return lax.fori_loop(0, number, column_turn, jnp.zeros_like(normal))

def solve_lower(factor, right):
    number = factor.shape[0]
    rows = jnp.arange(number, dtype=jnp.int32)

    def row_turn(index, result):
        index = index.astype(jnp.int32)
        select = (rows == index).astype(jnp.float32)
        own_row = jnp.dot(select, factor, precision=HIGHEST)
        pivot = jnp.dot(own_row, select, precision=HIGHEST)
        value = (jnp.dot(select, right, precision=HIGHEST) - jnp.dot(own_row, result, precision=HIGHEST)) / pivot
        return result + select[:, None] * value[None, :]
    return lax.fori_loop(0, number, row_turn, jnp.zeros_like(right))

def solve_upper_of(factor, right):
    number = factor.shape[0]
    rows = jnp.arange(number, dtype=jnp.int32)

    def row_turn(step, result):
        index = (number - 1 - step).astype(jnp.int32)
        select = (rows == index).astype(jnp.float32)
        own_row = jnp.dot(factor.T, select, precision=HIGHEST)
        pivot = jnp.dot(own_row, select, precision=HIGHEST)
        value = (jnp.dot(select, right, precision=HIGHEST) - jnp.dot(own_row, result, precision=HIGHEST)) / pivot
        return result + select[:, None] * value[None, :]
    return lax.fori_loop(0, number, row_turn, jnp.zeros_like(right))

def fit_matrix(points):
    number = points.shape[1]
    vectors = OUTER * points[:, :, None] - INNER * points[:, None, :]
    kernel = green(vectors[0], vectors[1], vectors[2])
    normal = jnp.dot(kernel.T, kernel, precision=HIGHEST)
    ridge = REGULAR * jnp.trace(normal) / number
    normal = normal + ridge * jnp.eye(number, dtype=jnp.float32)
    factor = factor_lower(normal)
    middle = solve_lower(factor, kernel.T)
    return solve_upper_of(factor, middle)

def child_table(points, downward):
    half = jnp.array([-0.5, 0.5], dtype=jnp.float32)
    if downward:
        vectors = INNER * points[:, :, None] - PARENT_CHECK * points[:, None, :]
        sign = 1.0
    else:
        vectors = PARENT_CHECK * points[:, :, None] - INNER * points[:, None, :]
        sign = -1.0
    first = vectors[0][None, None, None] + sign * half[:, None, None, None, None]
    second = vectors[1][None, None, None] + sign * half[None, :, None, None, None]
    third = vectors[2][None, None, None] + sign * half[None, None, :, None, None]
    first, second, third = jnp.broadcast_arrays(first, second, third)
    return green(first, second, third)

def multiply_fit(checks, fit):
    return jnp.einsum('...k,jk->...j', checks, fit, precision=HIGHEST)

def apply_down(checks, fit):
    return jnp.einsum('...k,kj->...j', checks, fit, precision=HIGHEST)

def lift(child, up_table, fit):
    a, b, c, q = child.shape
    grouped = child.reshape(a // 2, 2, b // 2, 2, c // 2, 2, q)
    checks = jnp.einsum('axbyczk,xyzjk->abcj', grouped, up_table, precision=HIGHEST)
    return 2.0 * multiply_fit(checks, fit)

def descend(parent, down_table):
    a, b, c, q = parent.shape
    checks = jnp.einsum('abck,xyzjk->axbyczj', parent, down_table, precision=HIGHEST)
    return checks.reshape(2 * a, 2 * b, 2 * c, q)

def split_particles(particles, counts):
    slots = particles.shape[-1] // 4
    positions = particles[..., :3 * slots].reshape(particles.shape[:-1] + (3, slots))
    present = jnp.arange(slots, dtype=jnp.int32) < counts[..., None]
    strengths = jnp.where(present, particles[..., 3 * slots:], 0.0)
    return (positions, strengths)

def upward_checks(positions, strengths, points):
    first = OUTER * points[0][:, None] - positions[..., 0, None, :]
    second = OUTER * points[1][:, None] - positions[..., 1, None, :]
    third = OUTER * points[2][:, None] - positions[..., 2, None, :]
    return lax.optimization_barrier(jnp.sum(green(first, second, third) * strengths[..., None, :], axis=-1))

def local_values(positions, densities, points):
    first = positions[..., 0, :, None] - OUTER * points[0]
    second = positions[..., 1, :, None] - OUTER * points[1]
    third = positions[..., 2, :, None] - OUTER * points[2]
    return lax.optimization_barrier(jnp.sum(green(first, second, third) * densities[..., None, :], axis=-1))

def pair_values(target_positions, source_positions, source_strengths, offset):
    first = target_positions[..., 0, :, None] - source_positions[..., 0, None, :] - offset[0]
    second = target_positions[..., 1, :, None] - source_positions[..., 1, None, :] - offset[1]
    third = target_positions[..., 2, :, None] - source_positions[..., 2, None, :] - offset[2]
    inverse = INV_FOUR_PI / jnp.sqrt(first * first + second * second + third * third + SOFTEN_SQUARED)
    return lax.optimization_barrier(jnp.sum(inverse * source_strengths[..., None, :], axis=-1))

def list_kernels(offsets, points):
    first = INNER * (points[0][:, None] - points[0][None, :]) - offsets[:, 0, None, None]
    second = INNER * (points[1][:, None] - points[1][None, :]) - offsets[:, 1, None, None]
    third = INNER * (points[2][:, None] - points[2][None, :]) - offsets[:, 2, None, None]
    return green(first, second, third)

def far_kernels(delta, points):
    base = INNER * (points[:, :, None] - points[:, None, :])
    first = delta[:, 0, None, None] + base[0]
    second = delta[:, 1, None, None] + base[1]
    third = delta[:, 2, None, None] + base[2]
    spread = lax.optimization_barrier(jnp.max(jnp.abs(delta), axis=1))
    return jnp.where((spread >= 2.0)[:, None, None], green(first, second, third), 0.0)

def allowed(shift, parity):
    return ((shift >= -2 - parity) & (shift <= 3 - parity)).astype(jnp.float32)

def list_level(multipoles, points):
    size_x, size_y, size_z, width = multipoles.shape
    padded = jnp.pad(multipoles, ((3, 3), (3, 3), (3, 3), (0, 0)))
    parity_x = jnp.arange(size_x, dtype=jnp.int32) % 2
    parity_y = jnp.arange(size_y, dtype=jnp.int32) % 2
    parity_z = jnp.arange(size_z, dtype=jnp.int32) % 2

    def list_turn(number, total):
        number = number.astype(jnp.int32)
        shift_x = number // 49
        shift_y = number // 7 % 7
        shift_z = number % 7
        block = lax.dynamic_slice(padded, (shift_x, shift_y, shift_z, jnp.int32(0)), (size_x, size_y, size_z, width))
        offset = jnp.stack([shift_x, shift_y, shift_z]).astype(jnp.float32) - 3.0
        spread = jnp.max(jnp.abs(offset))
        kernel = jnp.where(spread >= 2.0, list_kernels(offset[None, :], points)[0], 0.0)
        weights = allowed(shift_x - 3, parity_x)[:, None, None] * allowed(shift_y - 3, parity_y)[None, :, None] * allowed(shift_z - 3, parity_z)[None, None, :]
        product = jnp.dot(block.reshape(-1, width), kernel.T, precision=HIGHEST).reshape(size_x, size_y, size_z, width)
        return total + weights[..., None] * product
    return lax.fori_loop(0, 343, list_turn, jnp.zeros((size_x, size_y, size_z, width), jnp.float32))

def reference(particles, counts):
    points = sphere(Q)
    fit = fit_matrix(points)
    up_table = child_table(points, False)
    down_table = child_table(points, True)
    positions, strengths = split_particles(particles, counts)
    masked = jnp.concatenate([particles[..., :3 * P_SIZE], strengths], axis=3)
    leaf_checks = lax.map(lambda slab: upward_checks(slab[0], slab[1], points), (positions, strengths))
    leaf_multipoles = jnp.dot(leaf_checks.reshape(-1, Q), fit.T, precision=HIGHEST).reshape(NX, NY, NZ, Q)
    levels = SIDE.bit_length() - 1
    multipoles = [leaf_multipoles]
    for level in range(levels):
        multipoles.append(lift(multipoles[-1], up_table, fit))
    top = multipoles[levels]
    top_z = N_GZ * DEPTH
    top_rows = top.reshape(-1, Q)
    flat = jnp.arange(N_GX * N_GY * top_z, dtype=jnp.int32)
    coords = jnp.stack([flat // (N_GY * top_z), flat // top_z % N_GY, flat % top_z], axis=1).astype(jnp.float32)

    def one_target(target):
        kernels = far_kernels(target[None, :] - coords, points)
        return jnp.einsum('njk,nk->j', kernels, top_rows, precision=HIGHEST)
    far_checks = lax.map(one_target, coords)
    local = apply_down(far_checks, fit).reshape(N_GX, N_GY, top_z, Q)
    for level in range(levels - 1, -1, -1):
        local = apply_down(list_level(multipoles[level], points) + descend(local, down_table), fit)
    leaf_locals = local
    padded_near = jnp.pad(masked, ((1, 1), (1, 1), (1, 1), (0, 0)))

    def row_values(row):
        row = row.astype(jnp.int32)
        row_positions = lax.dynamic_index_in_dim(positions, row, 0, keepdims=False)
        row_locals = lax.dynamic_index_in_dim(leaf_locals, row, 0, keepdims=False)
        far_value = local_values(row_positions, row_locals, points)

        def near_turn(number, total):
            number = number.astype(jnp.int32)
            shift_x = number // 9
            shift_y = number // 3 % 3
            shift_z = number % 3
            block = lax.dynamic_slice(padded_near, (row + shift_x, shift_y, shift_z, jnp.int32(0)), (1, NY, NZ, 4 * P_SIZE))[0]
            source_positions = block[..., :3 * P_SIZE].reshape(NY, NZ, 3, P_SIZE)
            offset = jnp.stack([shift_x, shift_y, shift_z]).astype(jnp.float32) - 1.0
            return total + pair_values(row_positions, source_positions, block[..., 3 * P_SIZE:], offset)
        near_value = lax.fori_loop(0, 27, near_turn, jnp.zeros_like(far_value))
        return (far_value + near_value, near_value)
    values, near_values = lax.map(row_values, jnp.arange(NX, dtype=jnp.int32))
    return (values.reshape(NX, NY, NZ * P_SIZE), near_values.reshape(NX, NY, NZ * P_SIZE))
```

```python
import functools
import math

import jax
import jax.numpy as jnp
import ml_dtypes
import numpy as np
from jax import lax
from jax.experimental import pallas as pl
from jax.experimental.pallas import tpu as pltpu
from jax.sharding import PartitionSpec as P

Q = 64
INV_FOUR_PI = 0.07957747154594767
INNER = 0.9
OUTER = 1.5
PARENT_CHECK = 3.0
SOFTEN_SQUARED = 0.0625
REGULAR = 0.01
HIGHEST = lax.Precision.HIGHEST
MESH = pl.DeviceIdType.MESH
AXES = ("gx", "gy", "gz")


def sphere(number):
    order = np.arange(number, dtype=np.float64)
    height = 1.0 - (2.0 * order + 1.0) / number
    radial = np.sqrt(1.0 - height * height)
    turning = order * (math.pi * (3.0 - math.sqrt(5.0)))
    return np.stack([radial * np.cos(turning), radial * np.sin(turning), height])


def green(vectors):
    return INV_FOUR_PI / np.sqrt(np.sum(vectors * vectors, axis=0))


def constant_tables():
    points = sphere(Q)
    kernel = green(OUTER * points[:, :, None] - INNER * points[:, None, :])
    normal = kernel.T @ kernel
    normal = normal + REGULAR * np.trace(normal) / Q * np.eye(Q)
    lower = np.linalg.cholesky(normal)
    fit = np.linalg.solve(lower, kernel.T) / np.diag(lower)[:, None]
    up = np.zeros((8 * Q, Q))
    down = np.zeros((Q, 8 * Q))
    for child in range(8):
        offset = np.array([child // 4, child // 2 % 2, child % 2]) - 0.5
        vectors = PARENT_CHECK * points[:, :, None] - INNER * points[:, None, :]
        upper = green(vectors - offset[:, None, None])
        up[child * Q : (child + 1) * Q] = (2.0 * fit @ upper).T
        vectors = INNER * points[:, :, None] - PARENT_CHECK * points[:, None, :]
        lower = green(vectors + offset[:, None, None])
        down[:, child * Q : (child + 1) * Q] = lower.T @ fit
    base = INNER * (points[:, :, None] - points[:, None, :])
    table = np.zeros((7, 7, 6, Q, 2, Q), np.float32)
    for ox in range(-3, 4):
        for oy in range(-3, 4):
            for sz in range(6):
                for cz in range(2):
                    offset = np.array([ox, oy, sz - 2 - cz], np.float64)
                    if np.max(np.abs(offset)) >= 2:
                        values = green(base - offset[:, None, None])
                        table[ox + 3, oy + 3, sz, :, cz, :] = values.T
    table = table.reshape(7, 7, 6 * Q, 2 * Q)
    high = table.astype(ml_dtypes.bfloat16)
    low = (table - high.astype(np.float32)).astype(ml_dtypes.bfloat16)
    spread = np.repeat((OUTER * points)[:, :, None], 128, axis=2)
    single = np.float32
    return (
        spread.astype(single),
        np.tile(fit.T, (1, 2)).astype(single),
        np.tile(up, (1, 2)).astype(single),
        np.tile(base, (1, 1, 2)).astype(single),
        fit.astype(single),
        np.kron(np.eye(2), fit).astype(single),
        down.astype(single),
        high,
        low,
    )


def dot(left, right):
    return jnp.dot(left, right, precision=HIGHEST, preferred_element_type=jnp.float32)


def lanes(shape=(1, 128)):
    return lax.broadcasted_iota(jnp.int32, shape, 1)


def fused_kernel(
    sizes,
    part,
    counts,
    spread,
    fit_twice,
    up,
    base,
    fit,
    pair_fit,
    down,
    high_far,
    low_far,
    potential,
    near_out,
    cells,
    planes,
    own,
    rows,
    slab0,
    slab1,
    slab2,
    leaf,
    mid,
    coarse,
    tops,
    stage,
    lift_rows,
    pz_out,
    pz_in,
    my_out,
    my_in,
    gather,
    gather_mid,
    wide,
    narrow,
    total,
    near_sum,
    local,
    high,
    low,
    send_sem,
    recv_sem,
    table_sem,
):
    nx, ny, nz = sizes
    place = {axis: lax.axis_index(axis) for axis in AXES}
    count = dict(zip(AXES, sizes))
    mx, my, mz = (place[axis] for axis in AXES)
    half = lanes() < Q

    tables = [
        pltpu.make_async_copy(high_far, high, table_sem.at[0]),
        pltpu.make_async_copy(low_far, low, table_sem.at[1]),
    ]
    for table in tables:
        table.start()

    def clear(ref):
        def turn(number, carry):
            ref[number] = jnp.zeros(ref.shape[1:], jnp.float32)
            return carry

        lax.fori_loop(0, ref.shape[0], turn, 0)

    for ref in (cells, leaf, mid, coarse, my_out):
        clear(ref)

    barrier = pltpu.get_barrier_semaphore()
    mates = [
        (axis, lax.rem(place[axis] + step, count[axis]))
        for axis in AXES
        for step in range(1, count[axis])
    ]
    for axis, mate in mates:
        pl.semaphore_signal(barrier, inc=1, device_id={axis: mate}, device_id_type=MESH)

    class Shift:
        def __init__(self, axis, step, index, source, target):
            m, n = place[axis], count[axis]
            first, last = m > 0, m < n - 1
            self.sends, self.receives = (last, first) if step == 1 else (first, last)
            self.copy = pltpu.make_async_remote_copy(
                src_ref=source,
                dst_ref=target,
                send_sem=send_sem.at[index],
                recv_sem=recv_sem.at[index],
                device_id={axis: lax.rem(m + step + n, n)},
                device_id_type=MESH,
            )

        def start(self):
            pl.when(self.sends)(lambda: self.copy.start())

        def wait(self):
            pl.when(self.sends)(lambda: self.copy.wait_send())
            pl.when(self.receives)(lambda: self.copy.wait_recv())

    class Spread:
        def __init__(self, axis, step, index, block):
            m, n = place[axis], count[axis]
            self.copy = pltpu.make_async_remote_copy(
                src_ref=block,
                dst_ref=block,
                send_sem=send_sem.at[index],
                recv_sem=recv_sem.at[index],
                device_id={axis: lax.rem(m + step, n)},
                device_id_type=MESH,
            )

        def start(self):
            self.copy.start()

        def wait(self):
            self.copy.wait_send()
            self.copy.wait_recv()

    def start(copies):
        for copy in copies:
            copy.start()

    def wait(copies):
        for copy in copies:
            copy.wait()

    slot = lanes((8, 128)) - 96
    square = lax.broadcasted_iota(jnp.int32, (8, 8), 0) == lax.broadcasted_iota(jnp.int32, (8, 8), 1)

    def mask_turn(x, carry):
        present = counts[x].astype(jnp.float32)
        for y in range(8):
            line = jnp.where(square, jnp.broadcast_to(present[y : y + 1], (8, 8)), 0.0)
            number = jnp.sum(line, axis=1, keepdims=True)
            values = jnp.where(slot.astype(jnp.float32) < number, part[x, y], 0.0)
            cells[x + 1, 16 * (y + 1) + 1 : 16 * (y + 1) + 9, :] = values
        return carry

    lax.fori_loop(0, 8, mask_turn, 0)
    for x in range(8):
        for side, z in ((0, 8), (1, 1)):
            pz_out[side, 8 * x : 8 * x + 8, :] = cells[x + 1, pl.ds(16 + z, 8, stride=16), :]

    pl.semaphore_wait(barrier, len(mates))
    shifts = [Shift("gz", 1 - 2 * s, s, pz_out.at[s], pz_in.at[s]) for s in range(2)]
    start(shifts)

    def upward(b):
        pieces = [
            cells[2 * b + 1 + i, 16 * (y + 1) + 1 : 16 * (y + 1) + 9, :]
            for i in range(2)
            for y in range(8)
        ]
        turned = jnp.concatenate(pieces, axis=0).T
        own[b] = turned
        tx, ty, tz = turned[0:32], turned[32:64], turned[64:96]
        rows[0:96] = -2.0 * turned[0:96]
        rows[96:128] = turned[96:128] * INV_FOUR_PI
        rows[128:160] = (tx * tx + ty * ty) + (tz * tz + OUTER * OUTER)

        def slot_turn(p, value):
            distance = rows[pl.ds(128 + p, 1), :] + (
                spread[0] * rows[pl.ds(p, 1), :]
                + spread[1] * rows[pl.ds(32 + p, 1), :]
                + spread[2] * rows[pl.ds(64 + p, 1), :]
            )
            return value + lax.rsqrt(distance) * rows[pl.ds(96 + p, 1), :]

        checks = lax.fori_loop(0, 32, slot_turn, jnp.zeros((Q, 128), jnp.float32), unroll=4)
        stage[...] = dot(checks.T, fit_twice[...])
        for i in range(2):
            for pair in range(4):
                even = stage[pl.ds(64 * i + 2 * pair, 8, stride=8), :]
                odd = stage[pl.ds(64 * i + 2 * pair + 1, 8, stride=8), :]
                leaf[pair + 1, 2 * b + i + 2, 2:10, :] = jnp.where(half, even, odd)

    upward(0)
    upward(1)
    wait(shifts)

    @pl.when(mz > 0)
    def _():
        for x in range(8):
            cells[x + 1, pl.ds(16, 8, stride=16), :] = pz_in[0, 8 * x : 8 * x + 8, :]

    @pl.when(mz < nz - 1)
    def _():
        for x in range(8):
            cells[x + 1, pl.ds(16 + 9, 8, stride=16), :] = pz_in[1, 8 * x : 8 * x + 8, :]

    inner = pl.ds(1, 8)
    shifts = [
        Shift("gy", 1, 2, cells.at[inner, pl.ds(128, 16)], cells.at[inner, pl.ds(0, 16)]),
        Shift("gy", -1, 3, cells.at[inner, pl.ds(16, 16)], cells.at[inner, pl.ds(144, 16)]),
    ]
    start(shifts)
    upward(2)
    upward(3)
    wait(shifts)
    shifts = [
        Shift("gx", 1, 4, cells.at[8], cells.at[0]),
        Shift("gx", -1, 5, cells.at[1], cells.at[9]),
    ]
    start(shifts)

    for c in range(4):
        for z in range(4):
            for x in range(4):
                piece = leaf[z + 1, 2 * x + c // 2 + 2, pl.ds(c % 2 + 2, 4, stride=2), :]
                lift_rows[16 * z + 4 * x : 16 * z + 4 * x + 4, 128 * c : 128 * c + 128] = piece
    stage[0:64] = dot(lift_rows[...], up[...])
    for pair in range(2):
        for x in range(4):
            even = stage[32 * pair + 4 * x : 32 * pair + 4 * x + 4, :]
            odd = stage[32 * pair + 16 + 4 * x : 32 * pair + 16 + 4 * x + 4, :]
            mid[pair + 1, x + 2, 2:6, :] = jnp.where(half, even, odd)
    for c in range(4):
        for z in range(2):
            for x in range(2):
                piece = mid[z + 1, 2 * x + c // 2 + 2, pl.ds(c % 2 + 2, 2, stride=2), :]
                lift_rows[4 * z + 2 * x : 4 * z + 2 * x + 2, 128 * c : 128 * c + 128] = piece
    stage[0:8] = dot(lift_rows[0:8], up[...])
    for x in range(2):
        even, odd = stage[2 * x : 2 * x + 2, :], stage[4 + 2 * x : 4 + 2 * x + 2, :]
        coarse[1, x + 2, 2:4, :] = jnp.where(half, even, odd)
    line = jnp.concatenate(
        [coarse[1, c // 2 + 2, c % 2 + 2 : c % 2 + 3, :] for c in range(4)], axis=1
    )
    tops[mx, my, mz] = dot(jnp.broadcast_to(line, (8, 8 * Q)), up[...])

    multi = [
        Shift("gz", 1, 6, leaf.at[4, pl.ds(2, 8)], leaf.at[0, pl.ds(2, 8)]),
        Shift("gz", -1, 7, leaf.at[1, pl.ds(2, 8)], leaf.at[5, pl.ds(2, 8)]),
        Shift("gz", 1, 8, mid.at[2, pl.ds(2, 4)], mid.at[0, pl.ds(2, 4)]),
        Shift("gz", -1, 9, mid.at[1, pl.ds(2, 4)], mid.at[3, pl.ds(2, 4)]),
        Shift("gz", 1, 10, coarse.at[1, pl.ds(2, 2)], coarse.at[0, pl.ds(2, 2)]),
        Shift("gz", -1, 11, coarse.at[1, pl.ds(2, 2)], coarse.at[2, pl.ds(2, 2)]),
    ]
    index = 20
    for step in range(1, nz):
        multi.append(Spread("gz", step, index, tops.at[mx, my, mz]))
        index += 1
    start(multi)
    wait(shifts)

    def plane_turn(x, carry):
        for oz in range(3):
            pieces = [cells[x, 16 * y + oz : 16 * y + oz + 8, :] for y in range(10)]
            turned = jnp.concatenate(pieces + pieces[:6], axis=0).T
            sx, sy, sz = turned[0:32], turned[32:64], turned[64:96]
            planes[oz, x, 0:96] = turned[0:96]
            planes[oz, x, 96:128] = turned[96:128] * INV_FOUR_PI
            planes[oz, x, 128:160] = (sx * sx + sy * sy) + sz * sz
        return carry

    lax.fori_loop(0, 10, plane_turn, 0)

    slabs = (slab0, slab1, slab2)
    group = lanes((8, 128)) // 32

    def spread_out(values, target, b):
        stage[...] = jnp.concatenate([values] * 4, axis=0).T
        for i in range(2):
            for block in range(2):
                result = None
                for z in range(4):
                    line = stage[pl.ds(64 * i + 4 * block + z, 8, stride=8), :]
                    result = line if z == 0 else jnp.where(group == z, line, result)
                target[2 * b + i, :, 128 * block : 128 * block + 128] = result

    def near(b):
        turned = own[b]
        tx, ty, tz = -2.0 * turned[0:32], -2.0 * turned[32:64], -2.0 * turned[64:96]

        def fill(number, oy):
            x = 2 * b + number // 3
            oz = number % 3
            first = pltpu.roll(planes[oz, x], (128 - 8 * oy) % 128, 1)
            second = pltpu.roll(planes[oz, x + 1], (64 - 8 * oy) % 128, 1)
            slabs[oy][...] = jnp.where(half, first, second)

        for oy in range(3):
            fill(0, oy)

        def offset_turn(number, value):
            dx = tx + 2.0 * (number // 3 - 1).astype(jnp.float32)
            dz = tz + 2.0 * (number % 3 - 1).astype(jnp.float32)
            for oy in range(3):
                dy = ty + 2.0 * (oy - 1)
                squared = 0.25 * (dx * dx + dy * dy + dz * dz) + SOFTEN_SQUARED
                source = slabs[oy]

                def source_turn(p, value):
                    distance = (squared + source[pl.ds(128 + p, 1), :]) + (
                        dx * source[pl.ds(p, 1), :]
                        + dy * source[pl.ds(32 + p, 1), :]
                        + dz * source[pl.ds(64 + p, 1), :]
                    )
                    return value + lax.rsqrt(distance) * source[pl.ds(96 + p, 1), :]

                value = lax.fori_loop(0, 32, source_turn, value, unroll=32)
                fill(jnp.minimum(number + 1, 8), oy)
            return value

        value = lax.fori_loop(0, 9, offset_turn, jnp.zeros((32, 128), jnp.float32))
        near_sum[b] = value
        spread_out(value, near_out, b)

    near(0)
    wait(multi)
    at = 0
    packed = []
    for ref, tiles, width in ((leaf, 6, 8), (mid, 4, 4), (coarse, 3, 2)):
        for tile in range(tiles):
            for x in range(width):
                packed.append((ref, tile, x + 2, width))
    for number, (ref, tile, x, width) in enumerate(packed):
        my_out[0, 2 * number : 2 * number + 2, :] = ref[tile, x, width : width + 2, :]
        my_out[1, 2 * number : 2 * number + 2, :] = ref[tile, x, 2:4, :]
    multi = [Shift("gy", 1 - 2 * s, 12 + s, my_out.at[s], my_in.at[s]) for s in range(2)]
    for step in range(1, ny):
        multi.append(Spread("gy", step, index, tops.at[mx, my]))
        index += 1
    start(multi)
    near(1)
    wait(multi)

    @pl.when(my > 0)
    def _():
        for number, (ref, tile, x, width) in enumerate(packed):
            ref[tile, x, 0:2, :] = my_in[0, 2 * number : 2 * number + 2, :]

    @pl.when(my < ny - 1)
    def _():
        for number, (ref, tile, x, width) in enumerate(packed):
            ref[tile, x, width + 2 : width + 4, :] = my_in[1, 2 * number : 2 * number + 2, :]

    multi = []
    for number, (ref, tiles, width) in enumerate(((leaf, 6, 8), (mid, 4, 4), (coarse, 3, 2))):
        every = pl.ds(0, tiles)
        left, right = ref.at[every, pl.ds(0, 2)], ref.at[every, pl.ds(width + 2, 2)]
        multi.append(Shift("gx", 1, 14 + 2 * number, ref.at[every, pl.ds(width, 2)], left))
        multi.append(Shift("gx", -1, 15 + 2 * number, ref.at[every, pl.ds(2, 2)], right))
    for step in range(1, nx):
        multi.append(Spread("gx", step, index, tops.at[mx]))
        index += 1
    start(multi)
    near(2)
    wait(multi)
    near(3)

    def far_turn(number, value):
        sx = number // (ny * (nz // 2))
        sy = number // (nz // 2) % ny
        sz = 2 * (number % (nz // 2))
        row = jnp.where(half, tops[sx, sy, sz, 0:1, :], tops[sx, sy, sz + 1, 0:1, :])
        dx = (mx - sx).astype(jnp.float32)
        dy = (my - sy).astype(jnp.float32)
        dz = (mz - sz).astype(jnp.float32) - jnp.where(half, 0.0, 1.0)
        first, second, third = base[0] + dx, base[1] + dy, base[2] + dz
        squared = first * first + second * second + third * third
        reach = jnp.maximum(jnp.maximum(jnp.abs(dx), jnp.abs(dy)), jnp.abs(dz))
        weight = jnp.where(reach >= 2.0, row * INV_FOUR_PI, 0.0)
        kernel = jnp.where(reach >= 2.0, lax.rsqrt(squared), 0.0)
        return value + kernel * weight

    checks = lax.fori_loop(0, nx * ny * (nz // 2), far_turn, jnp.zeros((Q, 128), jnp.float32))
    top_local = jnp.sum(dot(checks.T, fit[...]), axis=0, keepdims=True)

    def split(values):
        first = values.astype(jnp.bfloat16)
        return first, (values - first.astype(jnp.float32)).astype(jnp.bfloat16)

    def wide_turn(ux, carry):
        for uy in range(8):
            for tile in range(6):
                for gx in range(2):
                    piece = leaf[tile, ux + 4 * gx, pl.ds(uy, 2, stride=4), :]
                    gather[uy, 4 * tile + 2 * gx : 4 * tile + 2 * gx + 2, :] = piece
        for uy in range(8):
            for t in range(3):
                first, second = split(gather[uy, 4 * t : 4 * t + 16, :])
                wide[0, ux, uy, :, 128 * t : 128 * t + 128] = first
                wide[1, ux, uy, :, 128 * t : 128 * t + 128] = second
        return carry

    lax.fori_loop(0, 8, wide_turn, 0)

    def narrow_turn(sx, carry):
        for sy in range(6):
            for tile in range(4):
                for gx in range(2):
                    piece = mid[tile, sx + 2 * gx, pl.ds(sy, 2, stride=2), :]
                    gather_mid[sy, 4 * tile + 2 * gx : 4 * tile + 2 * gx + 2, :] = piece
        for sy in range(6):
            for t in range(3):
                last = jnp.broadcast_to(coarse[t, sx, sy : sy + 1, :], (8, 128))
                both = jnp.concatenate([gather_mid[sy, 4 * t : 4 * t + 8, :], last], axis=0)
                first, second = split(both)
                narrow[0, sx, sy, :, 128 * t : 128 * t + 128] = first
                narrow[1, sx, sy, :, 128 * t : 128 * t + 128] = second
        return carry

    lax.fori_loop(0, 6, narrow_turn, 0)
    for table in tables:
        table.wait()
    total[...] = jnp.zeros_like(total)

    def list_turn(number, carry):
        sx = number // 3
        lefts, highs, lows = [], [], []
        for k in range(2):
            sy = 2 * (number % 3) + k
            columns = []
            for h in range(2):
                columns += [wide[h, sx + 2 * (c // 2), sy + 2 * (c % 2)] for c in range(4)]
                columns.append(narrow[h, sx, sy])
            lefts.append(jnp.concatenate(columns, axis=0))
            places = [(sx + 1 - c // 2, sy + 1 - c % 2) for c in range(4)]
            highs.append(jnp.concatenate([high[a, b] for a, b in places], axis=1))
            lows.append(jnp.concatenate([low[a, b] for a, b in places], axis=1))
        left = jnp.concatenate(lefts, axis=1)
        right_high = jnp.concatenate(highs, axis=0)
        right_low = jnp.concatenate(lows, axis=0)
        first = jnp.dot(left, right_high, preferred_element_type=jnp.float32)
        second = jnp.dot(left[:80], right_low, preferred_element_type=jnp.float32)
        total[...] += first[:80] + first[80:] + second
        return carry

    lax.fori_loop(0, 18, list_turn, 0)
    fitted = jnp.concatenate(
        [dot(total[:, 128 * pair : 128 * pair + 128], pair_fit[...]) for pair in range(4)], axis=1
    )
    line = fitted[72:80] + dot(jnp.broadcast_to(top_local, (8, Q)), down[...])
    order = [2 * c + z for z in range(2) for c in range(4)]
    boxes = jnp.concatenate([line[0:1, Q * c : Q * c + Q] for c in order], axis=0)
    boxes = fitted[64:72] + dot(boxes, down[...])
    for c in range(4):
        for z in range(4):
            column = Q * (2 * c + z % 2)
            stage[16 * c + 4 * z : 16 * c + 4 * z + 4, 0:Q] = boxes[
                4 * (z // 2) : 4 * (z // 2) + 4, column : column + Q
            ]
    lines = fitted[0:64] + dot(stage[0:64, 0:Q], down[...])
    for h in range(4):
        local[h] = lines[:, 128 * h : 128 * h + 128]

    even = lanes() % 2 == 0
    for b in range(4):
        for h in range(4):
            for cy in range(2):
                for gy in range(2):
                    start_row = 16 * (2 * (b % 2) + cy) + 2 * (b // 2) + gy
                    piece = local[h, pl.ds(start_row, 4, stride=4), :]
                    target = 64 * (h // 2) + 8 * (2 * (cy + 2 * gy) + h % 2)
                    stage[pl.ds(target, 4, stride=2), :] = piece
                    stage[pl.ds(target + 1, 4, stride=2), :] = piece
        turned = stage[...].T * INV_FOUR_PI
        rows[0:Q] = jnp.where(even, turned[0:Q], turned[Q : 2 * Q])
        position = own[b]
        tx, ty, tz = -2.0 * position[0:32], -2.0 * position[32:64], -2.0 * position[64:96]
        squared = 0.25 * (tx * tx + ty * ty + tz * tz) + OUTER * OUTER

        def point_turn(k, value):
            distance = squared + (
                tx * spread[0, pl.ds(k, 1), :]
                + ty * spread[1, pl.ds(k, 1), :]
                + tz * spread[2, pl.ds(k, 1), :]
            )
            return value + lax.rsqrt(distance) * rows[pl.ds(k, 1), :]

        value = lax.fori_loop(0, Q, point_turn, near_sum[b], unroll=16)
        spread_out(value, potential, b)


def per_device(particles, counts):
    spread, fit_twice, up, base, fit, pair_fit, down, high, low = constant_tables()
    sizes = tuple(lax.axis_size(axis) for axis in AXES)
    copies = 20 + sum(sizes) - 3
    vmem = pl.BlockSpec(memory_space=pltpu.VMEM)
    remote = pl.BlockSpec(memory_space=pl.ANY)
    single = jnp.float32

    def array(*shape):
        return pltpu.VMEM(shape, single)

    return pl.pallas_call(
        functools.partial(fused_kernel, sizes),
        out_shape=(jax.ShapeDtypeStruct((8, 8, 256), single),) * 2,
        in_specs=[vmem] * 9 + [remote] * 2,
        out_specs=(vmem, vmem),
        scratch_shapes=[
            array(10, 160, 128),
            array(3, 10, 160, 128),
            array(4, 128, 128),
            array(160, 128),
            array(160, 128),
            array(160, 128),
            array(160, 128),
            array(6, 12, 16, 128),
            array(4, 8, 8, 128),
            array(3, 6, 8, 128),
            array(*sizes, 8, 128),
            array(128, 128),
            array(64, 512),
            array(2, 64, 128),
            array(2, 64, 128),
            array(2, 144, 128),
            array(2, 144, 128),
            array(8, 24, 128),
            array(6, 16, 128),
            pltpu.VMEM((2, 8, 8, 16, 384), jnp.bfloat16),
            pltpu.VMEM((2, 6, 6, 16, 384), jnp.bfloat16),
            array(80, 512),
            array(4, 32, 128),
            array(4, 64, 128),
            pltpu.VMEM(high.shape, jnp.bfloat16),
            pltpu.VMEM(low.shape, jnp.bfloat16),
            pltpu.SemaphoreType.DMA((copies,)),
            pltpu.SemaphoreType.DMA((copies,)),
            pltpu.SemaphoreType.DMA((2,)),
        ],
        compiler_params=pltpu.CompilerParams(
            collective_id=0, has_side_effects=True, vmem_limit_bytes=56 << 20
        ),
        cost_estimate=pl.CostEstimate(flops=8 << 30, bytes_accessed=12 << 20, transcendentals=0),
    )(particles, counts, spread, fit_twice, up, base, fit, pair_fit, down, high, low)


def solution(mesh):
    placed = (P("gx", "gy", "gz", None), P("gx", "gy", "gz"))
    return jax.shard_map(
        per_device,
        mesh=mesh,
        in_specs=placed,
        out_specs=(P("gx", "gy", "gz"), P("gx", "gy", "gz")),
        check_vma=False,
    )
```

```python
import functools
import math

import jax
import jax.numpy as jnp
import ml_dtypes
import numpy as np
from jax import lax
from jax.experimental import pallas as pl
from jax.experimental.pallas import tpu as pltpu
from jax.sharding import PartitionSpec as P

Q = 64
INV_FOUR_PI = 0.07957747154594767
INNER = 0.9
OUTER = 1.5
PARENT_CHECK = 3.0
SOFTEN_SQUARED = 0.0625
REGULAR = 0.01
HIGHEST = lax.Precision.HIGHEST
MESH = pl.DeviceIdType.MESH
AXES = ("gx", "gy", "gz")


def sphere(number):
    order = np.arange(number, dtype=np.float64)
    height = 1.0 - (2.0 * order + 1.0) / number
    radial = np.sqrt(1.0 - height * height)
    turning = order * (math.pi * (3.0 - math.sqrt(5.0)))
    return np.stack([radial * np.cos(turning), radial * np.sin(turning), height])


def green(vectors):
    return INV_FOUR_PI / np.sqrt(np.sum(vectors * vectors, axis=0))


def constant_tables():
    points = sphere(Q)
    kernel = green(OUTER * points[:, :, None] - INNER * points[:, None, :])
    normal = kernel.T @ kernel
    normal = normal + REGULAR * np.trace(normal) / Q * np.eye(Q)
    lower = np.linalg.cholesky(normal)
    fit = np.linalg.solve(lower, kernel.T) / np.diag(lower)[:, None]
    up = np.zeros((8 * Q, Q))
    down = np.zeros((Q, 8 * Q))
    for child in range(8):
        offset = np.array([child // 4, child // 2 % 2, child % 2]) - 0.5
        vectors = PARENT_CHECK * points[:, :, None] - INNER * points[:, None, :]
        upper = green(vectors - offset[:, None, None])
        up[child * Q : (child + 1) * Q] = (2.0 * fit @ upper).T
        vectors = INNER * points[:, :, None] - PARENT_CHECK * points[:, None, :]
        lower = green(vectors + offset[:, None, None])
        down[:, child * Q : (child + 1) * Q] = lower.T @ fit
    base = INNER * (points[:, :, None] - points[:, None, :])
    table = np.zeros((7, 7, 6, Q, 2, Q), np.float32)
    for ox in range(-3, 4):
        for oy in range(-3, 4):
            for sz in range(6):
                for cz in range(2):
                    offset = np.array([ox, oy, sz - 2 - cz], np.float64)
                    if np.max(np.abs(offset)) >= 2:
                        values = green(base - offset[:, None, None])
                        table[ox + 3, oy + 3, sz, :, cz, :] = values.T
    table = table.reshape(7, 7, 6 * Q, 2 * Q)
    high = table.astype(ml_dtypes.bfloat16)
    low = (table - high.astype(np.float32)).astype(ml_dtypes.bfloat16)
    spread = np.repeat((OUTER * points)[:, :, None], 128, axis=2)
    single = np.float32
    return (
        spread.astype(single),
        np.tile(fit.T, (1, 2)).astype(single),
        np.tile(up, (1, 2)).astype(single),
        np.tile(base, (1, 1, 2)).astype(single),
        fit.astype(single),
        np.kron(np.eye(2), fit).astype(single),
        down.astype(single),
        high,
        low,
    )


def dot(left, right):
    return jnp.dot(left, right, precision=HIGHEST, preferred_element_type=jnp.float32)


def lanes(shape=(1, 128)):
    return lax.broadcasted_iota(jnp.int32, shape, 1)


def fused_kernel(
    sizes,
    part,
    counts,
    spread_far,
    fit_twice_far,
    up_far,
    base_far,
    fit_far,
    pair_fit_far,
    down_far,
    high_far,
    low_far,
    potential,
    near_out,
    spread,
    fit_twice,
    up,
    base,
    fit,
    pair_fit,
    down,
    cells,
    planes,
    own,
    rows,
    slab0,
    slab1,
    slab2,
    leaf,
    mid,
    coarse,
    tops_z,
    tops_y,
    tops,
    stage,
    lift_rows,
    pz_out,
    pz_in,
    my_out,
    my_in,
    gather,
    gather_mid,
    wide,
    narrow,
    total,
    near_sum,
    local,
    high,
    low,
    send_sem,
    recv_sem,
    table_sem,
):
    nx, ny, nz = sizes
    place = {axis: lax.axis_index(axis) for axis in AXES}
    count = dict(zip(AXES, sizes))
    mx, my, mz = (place[axis] for axis in AXES)
    half = lanes() < Q

    pairs = (
        (spread_far, spread),
        (fit_twice_far, fit_twice),
        (up_far, up),
        (base_far, base),
        (fit_far, fit),
        (pair_fit_far, pair_fit),
        (down_far, down),
        (high_far, high),
        (low_far, low),
    )
    tables = [
        pltpu.make_async_copy(far, here, table_sem.at[number])
        for number, (far, here) in enumerate(pairs)
    ]
    for table in tables:
        table.start()

    def clear(ref):
        def turn(number, carry):
            ref[number] = jnp.zeros(ref.shape[1:], jnp.float32)
            return carry

        lax.fori_loop(0, ref.shape[0], turn, 0)

    for ref in (cells, leaf, mid, coarse, my_out, tops_y, tops):
        clear(ref)

    barrier = pltpu.get_barrier_semaphore()
    mates = [
        (axis, lax.rem(place[axis] + step, count[axis]))
        for axis in AXES
        for step in range(1, count[axis])
    ]
    for axis, mate in mates:
        pl.semaphore_signal(barrier, inc=1, device_id={axis: mate}, device_id_type=MESH)

    class Shift:
        def __init__(self, axis, step, index, source, target):
            m, n = place[axis], count[axis]
            first, last = m > 0, m < n - 1
            self.sends, self.receives = (last, first) if step == 1 else (first, last)
            self.copy = pltpu.make_async_remote_copy(
                src_ref=source,
                dst_ref=target,
                send_sem=send_sem.at[index],
                recv_sem=recv_sem.at[index],
                device_id={axis: lax.rem(m + step + n, n)},
                device_id_type=MESH,
            )

        def start(self):
            pl.when(self.sends)(lambda: self.copy.start())

        def wait(self):
            pl.when(self.sends)(lambda: self.copy.wait_send())
            pl.when(self.receives)(lambda: self.copy.wait_recv())

    class Spread:
        def __init__(self, axis, step, index, block):
            m, n = place[axis], count[axis]
            self.copy = pltpu.make_async_remote_copy(
                src_ref=block,
                dst_ref=block,
                send_sem=send_sem.at[index],
                recv_sem=recv_sem.at[index],
                device_id={axis: lax.rem(m + step, n)},
                device_id_type=MESH,
            )

        def start(self):
            self.copy.start()

        def wait(self):
            self.copy.wait_send()
            self.copy.wait_recv()

    def start(copies):
        for copy in copies:
            copy.start()

    def wait(copies):
        for copy in copies:
            copy.wait()

    slot = lanes((8, 128)) - 96
    square = lax.broadcasted_iota(jnp.int32, (8, 8), 0) == lax.broadcasted_iota(jnp.int32, (8, 8), 1)

    def mask_turn(x, carry):
        present = counts[x].astype(jnp.float32)
        for y in range(8):
            line = jnp.where(square, jnp.broadcast_to(present[y : y + 1], (8, 8)), 0.0)
            number = jnp.sum(line, axis=1, keepdims=True)
            values = jnp.where(slot.astype(jnp.float32) < number, part[x, y], 0.0)
            cells[x + 1, 16 * (y + 1) + 1 : 16 * (y + 1) + 9, :] = values
        return carry

    lax.fori_loop(0, 8, mask_turn, 0)
    for x in range(8):
        for side, z in ((0, 8), (1, 1)):
            pz_out[side, 8 * x : 8 * x + 8, :] = cells[x + 1, pl.ds(16 + z, 8, stride=16), :]

    def upward(b):
        pieces = [
            cells[2 * b + 1 + i, 16 * (y + 1) + 1 : 16 * (y + 1) + 9, :]
            for i in range(2)
            for y in range(8)
        ]
        turned = jnp.concatenate(pieces, axis=0).T
        own[b] = turned
        tx, ty, tz = turned[0:32], turned[32:64], turned[64:96]
        rows[0:96] = -2.0 * turned[0:96]
        rows[96:128] = turned[96:128] * INV_FOUR_PI
        rows[128:160] = (tx * tx + ty * ty) + (tz * tz + OUTER * OUTER)

        def slot_turn(p, value):
            distance = rows[pl.ds(128 + p, 1), :] + (
                spread[0] * rows[pl.ds(p, 1), :]
                + spread[1] * rows[pl.ds(32 + p, 1), :]
                + spread[2] * rows[pl.ds(64 + p, 1), :]
            )
            return value + lax.rsqrt(distance) * rows[pl.ds(96 + p, 1), :]

        checks = lax.fori_loop(0, 32, slot_turn, jnp.zeros((Q, 128), jnp.float32), unroll=4)
        stage[...] = dot(checks.T, fit_twice[...])
        for i in range(2):
            for pair in range(4):
                even = stage[pl.ds(64 * i + 2 * pair, 8, stride=8), :]
                odd = stage[pl.ds(64 * i + 2 * pair + 1, 8, stride=8), :]
                leaf[pair + 1, 2 * b + i + 2, 2:10, :] = jnp.where(half, even, odd)

    tables[0].wait()
    tables[1].wait()
    upward(0)
    pl.semaphore_wait(barrier, len(mates))
    shifts = [Shift("gz", 1 - 2 * s, s, pz_out.at[s], pz_in.at[s]) for s in range(2)]
    start(shifts)
    upward(1)
    wait(shifts)

    @pl.when(mz > 0)
    def _():
        for x in range(8):
            cells[x + 1, pl.ds(16, 8, stride=16), :] = pz_in[0, 8 * x : 8 * x + 8, :]

    @pl.when(mz < nz - 1)
    def _():
        for x in range(8):
            cells[x + 1, pl.ds(16 + 9, 8, stride=16), :] = pz_in[1, 8 * x : 8 * x + 8, :]

    inner = pl.ds(1, 8)
    shifts = [
        Shift("gy", 1, 2, cells.at[inner, pl.ds(128, 16)], cells.at[inner, pl.ds(0, 16)]),
        Shift("gy", -1, 3, cells.at[inner, pl.ds(16, 16)], cells.at[inner, pl.ds(144, 16)]),
    ]
    start(shifts)
    upward(2)
    upward(3)
    tables[2].wait()

    for c in range(4):
        for z in range(4):
            for x in range(4):
                piece = leaf[z + 1, 2 * x + c // 2 + 2, pl.ds(c % 2 + 2, 4, stride=2), :]
                lift_rows[16 * z + 4 * x : 16 * z + 4 * x + 4, 128 * c : 128 * c + 128] = piece
    stage[0:64] = dot(lift_rows[...], up[...])
    for pair in range(2):
        for x in range(4):
            even = stage[32 * pair + 4 * x : 32 * pair + 4 * x + 4, :]
            odd = stage[32 * pair + 16 + 4 * x : 32 * pair + 16 + 4 * x + 4, :]
            mid[pair + 1, x + 2, 2:6, :] = jnp.where(half, even, odd)
    for c in range(4):
        for z in range(2):
            for x in range(2):
                piece = mid[z + 1, 2 * x + c // 2 + 2, pl.ds(c % 2 + 2, 2, stride=2), :]
                lift_rows[4 * z + 2 * x : 4 * z + 2 * x + 2, 128 * c : 128 * c + 128] = piece
    stage[0:8] = dot(lift_rows[0:8], up[...])
    for x in range(2):
        even, odd = stage[2 * x : 2 * x + 2, :], stage[4 + 2 * x : 4 + 2 * x + 2, :]
        coarse[1, x + 2, 2:4, :] = jnp.where(half, even, odd)
    line = jnp.concatenate(
        [coarse[1, c // 2 + 2, c % 2 + 2 : c % 2 + 3, :] for c in range(4)], axis=1
    )
    tops_z[mz] = dot(jnp.broadcast_to(line, (8, 8 * Q)), up[...])

    multi = [
        Shift("gz", 1, 6, leaf.at[4, pl.ds(2, 8)], leaf.at[0, pl.ds(2, 8)]),
        Shift("gz", -1, 7, leaf.at[1, pl.ds(2, 8)], leaf.at[5, pl.ds(2, 8)]),
        Shift("gz", 1, 8, mid.at[2, pl.ds(2, 4)], mid.at[0, pl.ds(2, 4)]),
        Shift("gz", -1, 9, mid.at[1, pl.ds(2, 4)], mid.at[3, pl.ds(2, 4)]),
        Shift("gz", 1, 10, coarse.at[1, pl.ds(2, 2)], coarse.at[0, pl.ds(2, 2)]),
        Shift("gz", -1, 11, coarse.at[1, pl.ds(2, 2)], coarse.at[2, pl.ds(2, 2)]),
    ]
    index = 20
    for step in range(1, nz):
        multi.append(Spread("gz", step, index, tops_z.at[mz]))
        index += 1
    start(multi)
    wait(shifts)
    shifts = [
        Shift("gx", 1, 4, cells.at[8], cells.at[0]),
        Shift("gx", -1, 5, cells.at[1], cells.at[9]),
    ]
    start(shifts)

    def plane_turn(x, carry):
        for oz in range(3):
            pieces = [cells[x, 16 * y + oz : 16 * y + oz + 8, :] for y in range(10)]
            turned = jnp.concatenate(pieces + pieces[:6], axis=0).T
            sx, sy, sz = turned[0:32], turned[32:64], turned[64:96]
            planes[oz, x, 0:96] = turned[0:96]
            planes[oz, x, 96:128] = turned[96:128] * INV_FOUR_PI
            planes[oz, x, 128:160] = (sx * sx + sy * sy) + sz * sz
        return carry

    lax.fori_loop(1, 9, plane_turn, 0)

    slabs = (slab0, slab1, slab2)
    group = lanes((8, 128)) // 32

    def spread_out(values, target, b):
        stage[...] = jnp.concatenate([values] * 4, axis=0).T
        for i in range(2):
            for block in range(2):
                result = None
                for z in range(4):
                    line = stage[pl.ds(64 * i + 4 * block + z, 8, stride=8), :]
                    result = line if z == 0 else jnp.where(group == z, line, result)
                target[2 * b + i, :, 128 * block : 128 * block + 128] = result

    def near(b):
        turned = own[b]
        tx, ty, tz = -2.0 * turned[0:32], -2.0 * turned[32:64], -2.0 * turned[64:96]

        def fill(number, oy):
            x = 2 * b + number // 3
            oz = number % 3
            first = pltpu.roll(planes[oz, x], (128 - 8 * oy) % 128, 1)
            second = pltpu.roll(planes[oz, x + 1], (64 - 8 * oy) % 128, 1)
            slabs[oy][...] = jnp.where(half, first, second)

        for oy in range(3):
            fill(0, oy)

        def offset_turn(number, value):
            dx = tx + 2.0 * (number // 3 - 1).astype(jnp.float32)
            dz = tz + 2.0 * (number % 3 - 1).astype(jnp.float32)
            for oy in range(3):
                dy = ty + 2.0 * (oy - 1)
                squared = 0.25 * (dx * dx + dy * dy + dz * dz) + SOFTEN_SQUARED
                source = slabs[oy]

                def source_turn(p, value):
                    distance = (squared + source[pl.ds(128 + p, 1), :]) + (
                        dx * source[pl.ds(p, 1), :]
                        + dy * source[pl.ds(32 + p, 1), :]
                        + dz * source[pl.ds(64 + p, 1), :]
                    )
                    return value + lax.rsqrt(distance) * source[pl.ds(96 + p, 1), :]

                value = lax.fori_loop(0, 32, source_turn, value, unroll=32)
                fill(jnp.minimum(number + 1, 8), oy)
            return value

        value = lax.fori_loop(0, 9, offset_turn, jnp.zeros((32, 128), jnp.float32))
        near_sum[b] = value
        spread_out(value, near_out, b)

    near(1)
    wait(multi)
    for pair in range(nz // 2):
        even, odd = tops_z[2 * pair, 0:1, :], tops_z[2 * pair + 1, 0:1, :]
        tops_y[my, pair : pair + 1, :] = jnp.where(half, even, odd)
    packed = []
    for ref, tiles, width in ((leaf, 6, 8), (mid, 4, 4), (coarse, 3, 2)):
        for tile in range(tiles):
            for x in range(width):
                packed.append((ref, tile, x + 2, width))
    for number, (ref, tile, x, width) in enumerate(packed):
        my_out[0, 2 * number : 2 * number + 2, :] = ref[tile, x, width : width + 2, :]
        my_out[1, 2 * number : 2 * number + 2, :] = ref[tile, x, 2:4, :]
    multi = [Shift("gy", 1 - 2 * s, 12 + s, my_out.at[s], my_in.at[s]) for s in range(2)]
    for step in range(1, ny):
        multi.append(Spread("gy", step, index, tops_y.at[my]))
        index += 1
    start(multi)
    near(2)
    wait(multi)
    for y in range(ny):
        tops[mx, y * (nz // 2) : (y + 1) * (nz // 2), :] = tops_y[y, 0 : nz // 2, :]

    @pl.when(my > 0)
    def _():
        for number, (ref, tile, x, width) in enumerate(packed):
            ref[tile, x, 0:2, :] = my_in[0, 2 * number : 2 * number + 2, :]

    @pl.when(my < ny - 1)
    def _():
        for number, (ref, tile, x, width) in enumerate(packed):
            ref[tile, x, width + 2 : width + 4, :] = my_in[1, 2 * number : 2 * number + 2, :]

    multi = []
    for number, (ref, tiles, width) in enumerate(((leaf, 6, 8), (mid, 4, 4), (coarse, 3, 2))):
        every = pl.ds(0, tiles)
        left, right = ref.at[every, pl.ds(0, 2)], ref.at[every, pl.ds(width + 2, 2)]
        multi.append(Shift("gx", 1, 14 + 2 * number, ref.at[every, pl.ds(width, 2)], left))
        multi.append(Shift("gx", -1, 15 + 2 * number, ref.at[every, pl.ds(2, 2)], right))
    for step in range(1, nx):
        multi.append(Spread("gx", step, index, tops.at[mx]))
        index += 1
    start(multi)
    wait(shifts)
    plane_turn(0, 0)
    plane_turn(9, 0)
    near(0)
    near(3)
    wait(multi)
    for table in tables[3:]:
        table.wait()

    def far_turn(number, value):
        sx = number // (ny * (nz // 2))
        sy = number // (nz // 2) % ny
        sz = 2 * (number % (nz // 2))
        row = tops[sx, pl.ds(number % (ny * (nz // 2)), 1), :]
        dx = (mx - sx).astype(jnp.float32)
        dy = (my - sy).astype(jnp.float32)
        dz = (mz - sz).astype(jnp.float32) - jnp.where(half, 0.0, 1.0)
        first, second, third = base[0] + dx, base[1] + dy, base[2] + dz
        squared = first * first + second * second + third * third
        reach = jnp.maximum(jnp.maximum(jnp.abs(dx), jnp.abs(dy)), jnp.abs(dz))
        weight = jnp.where(reach >= 2.0, row * INV_FOUR_PI, 0.0)
        kernel = jnp.where(reach >= 2.0, lax.rsqrt(squared), 0.0)
        return value + kernel * weight

    checks = lax.fori_loop(0, nx * ny * (nz // 2), far_turn, jnp.zeros((Q, 128), jnp.float32))
    top_local = jnp.sum(dot(checks.T, fit[...]), axis=0, keepdims=True)

    def split(values):
        first = values.astype(jnp.bfloat16)
        return first, (values - first.astype(jnp.float32)).astype(jnp.bfloat16)

    def wide_turn(ux, carry):
        for uy in range(8):
            for tile in range(6):
                for gx in range(2):
                    piece = leaf[tile, ux + 4 * gx, pl.ds(uy, 2, stride=4), :]
                    gather[uy, 4 * tile + 2 * gx : 4 * tile + 2 * gx + 2, :] = piece
        for uy in range(8):
            for t in range(3):
                first, second = split(gather[uy, 4 * t : 4 * t + 16, :])
                wide[0, ux, uy, :, 128 * t : 128 * t + 128] = first
                wide[1, ux, uy, :, 128 * t : 128 * t + 128] = second
        return carry

    lax.fori_loop(0, 8, wide_turn, 0)

    def narrow_turn(sx, carry):
        for sy in range(6):
            for tile in range(4):
                for gx in range(2):
                    piece = mid[tile, sx + 2 * gx, pl.ds(sy, 2, stride=2), :]
                    gather_mid[sy, 4 * tile + 2 * gx : 4 * tile + 2 * gx + 2, :] = piece
        for sy in range(6):
            for t in range(3):
                last = jnp.broadcast_to(coarse[t, sx, sy : sy + 1, :], (8, 128))
                both = jnp.concatenate([gather_mid[sy, 4 * t : 4 * t + 8, :], last], axis=0)
                first, second = split(both)
                narrow[0, sx, sy, :, 128 * t : 128 * t + 128] = first
                narrow[1, sx, sy, :, 128 * t : 128 * t + 128] = second
        return carry

    lax.fori_loop(0, 6, narrow_turn, 0)
    total[...] = jnp.zeros_like(total)

    def list_turn(number, carry):
        sx = number // 3
        lefts, highs, lows = [], [], []
        for k in range(2):
            sy = 2 * (number % 3) + k
            columns = []
            for h in range(2):
                columns += [wide[h, sx + 2 * (c // 2), sy + 2 * (c % 2)] for c in range(4)]
                columns.append(narrow[h, sx, sy])
            lefts.append(jnp.concatenate(columns, axis=0))
            places = [(sx + 1 - c // 2, sy + 1 - c % 2) for c in range(4)]
            highs.append(jnp.concatenate([high[a, b] for a, b in places], axis=1))
            lows.append(jnp.concatenate([low[a, b] for a, b in places], axis=1))
        left = jnp.concatenate(lefts, axis=1)
        right_high = jnp.concatenate(highs, axis=0)
        right_low = jnp.concatenate(lows, axis=0)
        first = jnp.dot(left, right_high, preferred_element_type=jnp.float32)
        second = jnp.dot(left[:80], right_low, preferred_element_type=jnp.float32)
        total[...] += first[:80] + first[80:] + second
        return carry

    lax.fori_loop(0, 18, list_turn, 0)
    fitted = jnp.concatenate(
        [dot(total[:, 128 * pair : 128 * pair + 128], pair_fit[...]) for pair in range(4)], axis=1
    )
    line = fitted[72:80] + dot(jnp.broadcast_to(top_local, (8, Q)), down[...])
    order = [2 * c + z for z in range(2) for c in range(4)]
    boxes = jnp.concatenate([line[0:1, Q * c : Q * c + Q] for c in order], axis=0)
    boxes = fitted[64:72] + dot(boxes, down[...])
    for c in range(4):
        for z in range(4):
            column = Q * (2 * c + z % 2)
            stage[16 * c + 4 * z : 16 * c + 4 * z + 4, 0:Q] = boxes[
                4 * (z // 2) : 4 * (z // 2) + 4, column : column + Q
            ]
    lines = fitted[0:64] + dot(stage[0:64, 0:Q], down[...])
    for h in range(4):
        local[h] = lines[:, 128 * h : 128 * h + 128]

    even = lanes() % 2 == 0
    for b in range(4):
        for h in range(4):
            for cy in range(2):
                for gy in range(2):
                    start_row = 16 * (2 * (b % 2) + cy) + 2 * (b // 2) + gy
                    piece = local[h, pl.ds(start_row, 4, stride=4), :]
                    target = 64 * (h // 2) + 8 * (2 * (cy + 2 * gy) + h % 2)
                    stage[pl.ds(target, 4, stride=2), :] = piece
                    stage[pl.ds(target + 1, 4, stride=2), :] = piece
        turned = stage[...].T * INV_FOUR_PI
        rows[0:Q] = jnp.where(even, turned[0:Q], turned[Q : 2 * Q])
        position = own[b]
        tx, ty, tz = -2.0 * position[0:32], -2.0 * position[32:64], -2.0 * position[64:96]
        squared = 0.25 * (tx * tx + ty * ty + tz * tz) + OUTER * OUTER

        def point_turn(k, value):
            distance = squared + (
                tx * spread[0, pl.ds(k, 1), :]
                + ty * spread[1, pl.ds(k, 1), :]
                + tz * spread[2, pl.ds(k, 1), :]
            )
            return value + lax.rsqrt(distance) * rows[pl.ds(k, 1), :]

        value = lax.fori_loop(0, Q, point_turn, near_sum[b], unroll=16)
        spread_out(value, potential, b)


def per_device(particles, counts):
    spread, fit_twice, up, base, fit, pair_fit, down, high, low = constant_tables()
    sizes = tuple(lax.axis_size(axis) for axis in AXES)
    nx, ny, nz = sizes
    copies = 20 + sum(sizes) - 3
    vmem = pl.BlockSpec(memory_space=pltpu.VMEM)
    remote = pl.BlockSpec(memory_space=pl.ANY)
    single = jnp.float32

    def array(*shape):
        return pltpu.VMEM(shape, single)

    return pl.pallas_call(
        functools.partial(fused_kernel, sizes),
        out_shape=(jax.ShapeDtypeStruct((8, 8, 256), single),) * 2,
        in_specs=[vmem] * 2 + [remote] * 9,
        out_specs=(vmem, vmem),
        scratch_shapes=[
            array(*spread.shape),
            array(*fit_twice.shape),
            array(*up.shape),
            array(*base.shape),
            array(*fit.shape),
            array(*pair_fit.shape),
            array(*down.shape),
            array(10, 160, 128),
            array(3, 10, 160, 128),
            array(4, 128, 128),
            array(160, 128),
            array(160, 128),
            array(160, 128),
            array(160, 128),
            array(6, 12, 16, 128),
            array(4, 8, 8, 128),
            array(3, 6, 8, 128),
            array(nz, 8, 128),
            array(ny, -(-nz // 16) * 8, 128),
            array(nx, -(-ny * nz // 16) * 8, 128),
            array(128, 128),
            array(64, 512),
            array(2, 64, 128),
            array(2, 64, 128),
            array(2, 144, 128),
            array(2, 144, 128),
            array(8, 24, 128),
            array(6, 16, 128),
            pltpu.VMEM((2, 8, 8, 16, 384), jnp.bfloat16),
            pltpu.VMEM((2, 6, 6, 16, 384), jnp.bfloat16),
            array(80, 512),
            array(4, 32, 128),
            array(4, 64, 128),
            pltpu.VMEM(high.shape, jnp.bfloat16),
            pltpu.VMEM(low.shape, jnp.bfloat16),
            pltpu.SemaphoreType.DMA((copies,)),
            pltpu.SemaphoreType.DMA((copies,)),
            pltpu.SemaphoreType.DMA((9,)),
        ],
        compiler_params=pltpu.CompilerParams(
            collective_id=0, has_side_effects=True, vmem_limit_bytes=56 << 20
        ),
        cost_estimate=pl.CostEstimate(flops=8 << 30, bytes_accessed=12 << 20, transcendentals=0),
    )(particles, counts, spread, fit_twice, up, base, fit, pair_fit, down, high, low)


def solution(mesh):
    placed = (P("gx", "gy", "gz", None), P("gx", "gy", "gz"))
    return jax.shard_map(
        per_device,
        mesh=mesh,
        in_specs=placed,
        out_specs=(P("gx", "gy", "gz"), P("gx", "gy", "gz")),
        check_vma=False,
    )
```

```python
import functools
import math

import jax
import jax.numpy as jnp
import ml_dtypes
import numpy as np
from jax import lax
from jax.experimental import pallas as pl
from jax.experimental.pallas import tpu as pltpu
from jax.sharding import PartitionSpec as P

Q = 64
INV_FOUR_PI = 0.07957747154594767
INNER = 0.9
OUTER = 1.5
PARENT_CHECK = 3.0
SOFTEN_SQUARED = 0.0625
REGULAR = 0.01
HIGHEST = lax.Precision.HIGHEST
MESH = pl.DeviceIdType.MESH
AXES = ("gx", "gy", "gz")


def sphere(number):
    order = np.arange(number, dtype=np.float64)
    height = 1.0 - (2.0 * order + 1.0) / number
    radial = np.sqrt(1.0 - height * height)
    turning = order * (math.pi * (3.0 - math.sqrt(5.0)))
    return np.stack([radial * np.cos(turning), radial * np.sin(turning), height])


def green(vectors):
    return INV_FOUR_PI / np.sqrt(np.sum(vectors * vectors, axis=0))


def constant_tables():
    points = sphere(Q)
    kernel = green(OUTER * points[:, :, None] - INNER * points[:, None, :])
    normal = kernel.T @ kernel
    normal = normal + REGULAR * np.trace(normal) / Q * np.eye(Q)
    lower = np.linalg.cholesky(normal)
    fit = np.linalg.solve(lower, kernel.T) / np.diag(lower)[:, None]
    up = np.zeros((8 * Q, Q))
    down = np.zeros((Q, 8 * Q))
    for child in range(8):
        offset = np.array([child // 4, child // 2 % 2, child % 2]) - 0.5
        vectors = PARENT_CHECK * points[:, :, None] - INNER * points[:, None, :]
        upper = green(vectors - offset[:, None, None])
        up[child * Q : (child + 1) * Q] = (2.0 * fit @ upper).T
        vectors = INNER * points[:, :, None] - PARENT_CHECK * points[:, None, :]
        lower = green(vectors + offset[:, None, None])
        down[:, child * Q : (child + 1) * Q] = lower.T @ fit
    base = INNER * (points[:, :, None] - points[:, None, :])
    table = np.zeros((7, 7, 6, Q, 2, Q), np.float32)
    for ox in range(-3, 4):
        for oy in range(-3, 4):
            for sz in range(6):
                for cz in range(2):
                    offset = np.array([ox, oy, sz - 2 - cz], np.float64)
                    if np.max(np.abs(offset)) >= 2:
                        values = green(base - offset[:, None, None])
                        table[ox + 3, oy + 3, sz, :, cz, :] = values.T
    table = table.reshape(7, 7, 6 * Q, 2 * Q)
    high = table.astype(ml_dtypes.bfloat16)
    low = (table - high.astype(np.float32)).astype(ml_dtypes.bfloat16)
    spread = np.repeat((OUTER * points)[:, :, None], 128, axis=2)
    single = np.float32
    return (
        spread.astype(single),
        np.tile(fit.T, (1, 2)).astype(single),
        np.tile(up, (1, 2)).astype(single),
        np.tile(base, (1, 1, 2)).astype(single),
        fit.astype(single),
        np.kron(np.eye(2), fit).astype(single),
        down.astype(single),
        high,
        low,
    )


def dot(left, right):
    return jnp.dot(left, right, precision=HIGHEST, preferred_element_type=jnp.float32)


def lanes(shape=(1, 128)):
    return lax.broadcasted_iota(jnp.int32, shape, 1)


def fused_kernel(
    sizes,
    part,
    counts,
    spread_far,
    fit_twice_far,
    up_far,
    base_far,
    fit_far,
    pair_fit_far,
    down_far,
    high_far,
    low_far,
    potential,
    near_out,
    spread,
    fit_twice,
    up,
    base,
    fit,
    pair_fit,
    down,
    cells,
    planes,
    edges,
    own,
    own_twice,
    rows,
    slab0,
    slab1,
    slab2,
    slab3,
    leaf,
    mid,
    coarse,
    tops_z,
    tops_y,
    tops,
    stage,
    lift_rows,
    pz_out,
    pz_in,
    my_out,
    my_in,
    gather,
    gather_mid,
    wide,
    narrow,
    total,
    near_sum,
    local,
    high,
    low,
    send_sem,
    recv_sem,
    table_sem,
):
    nx, ny, nz = sizes
    place = {axis: lax.axis_index(axis) for axis in AXES}
    count = dict(zip(AXES, sizes))
    mx, my, mz = (place[axis] for axis in AXES)
    half = lanes() < Q

    pairs = (
        (spread_far, spread),
        (fit_twice_far, fit_twice),
        (up_far, up),
        (base_far, base),
        (fit_far, fit),
        (pair_fit_far, pair_fit),
        (down_far, down),
        (high_far, high),
        (low_far, low),
    )
    tables = [
        pltpu.make_async_copy(far, here, table_sem.at[number])
        for number, (far, here) in enumerate(pairs)
    ]
    for table in tables:
        table.start()

    def clear(ref):
        def turn(number, carry):
            ref[number] = jnp.zeros(ref.shape[1:], jnp.float32)
            return carry

        lax.fori_loop(0, ref.shape[0], turn, 0)

    for ref in (cells, leaf, mid, coarse, my_out, tops_y, tops):
        clear(ref)

    barrier = pltpu.get_barrier_semaphore()
    mates = [
        (axis, lax.rem(place[axis] + step, count[axis]))
        for axis in AXES
        for step in range(1, count[axis])
    ]
    for axis, mate in mates:
        pl.semaphore_signal(barrier, inc=1, device_id={axis: mate}, device_id_type=MESH)

    class Shift:
        def __init__(self, axis, step, index, source, target):
            m, n = place[axis], count[axis]
            first, last = m > 0, m < n - 1
            self.sends, self.receives = (last, first) if step == 1 else (first, last)
            self.copy = pltpu.make_async_remote_copy(
                src_ref=source,
                dst_ref=target,
                send_sem=send_sem.at[index],
                recv_sem=recv_sem.at[index],
                device_id={axis: lax.rem(m + step + n, n)},
                device_id_type=MESH,
            )

        def start(self):
            pl.when(self.sends)(lambda: self.copy.start())

        def wait(self):
            pl.when(self.sends)(lambda: self.copy.wait_send())
            pl.when(self.receives)(lambda: self.copy.wait_recv())

    class Spread:
        def __init__(self, axis, step, index, block):
            m, n = place[axis], count[axis]
            self.copy = pltpu.make_async_remote_copy(
                src_ref=block,
                dst_ref=block,
                send_sem=send_sem.at[index],
                recv_sem=recv_sem.at[index],
                device_id={axis: lax.rem(m + step, n)},
                device_id_type=MESH,
            )

        def start(self):
            self.copy.start()

        def wait(self):
            self.copy.wait_send()
            self.copy.wait_recv()

    def start(copies):
        for copy in copies:
            copy.start()

    def wait(copies):
        for copy in copies:
            copy.wait()

    slot = lanes((8, 128)) - 96
    square = lax.broadcasted_iota(jnp.int32, (8, 8), 0) == lax.broadcasted_iota(jnp.int32, (8, 8), 1)

    def mask_turn(x, carry):
        present = counts[x].astype(jnp.float32)
        for y in range(8):
            line = jnp.where(square, jnp.broadcast_to(present[y : y + 1], (8, 8)), 0.0)
            number = jnp.sum(line, axis=1, keepdims=True)
            values = jnp.where(slot.astype(jnp.float32) < number, part[x, y], 0.0)
            cells[x + 1, 16 * (y + 1) + 1 : 16 * (y + 1) + 9, :] = values
        return carry

    lax.fori_loop(0, 8, mask_turn, 0)
    for x in range(8):
        for side, z in ((0, 8), (1, 1)):
            pz_out[side, 8 * x : 8 * x + 8, :] = cells[x + 1, pl.ds(16 + z, 8, stride=16), :]

    def upward(b):
        pieces = [
            cells[2 * b + 1 + i, 16 * (y + 1) + 1 : 16 * (y + 1) + 9, :]
            for i in range(2)
            for y in range(8)
        ]
        turned = jnp.concatenate(pieces, axis=0).T
        own[b] = turned
        own_twice[b] = -2.0 * turned[0:96]
        tx, ty, tz = turned[0:32], turned[32:64], turned[64:96]
        rows[0:96] = -2.0 * turned[0:96]
        rows[96:128] = turned[96:128] * INV_FOUR_PI
        rows[128:160] = (tx * tx + ty * ty) + (tz * tz + OUTER * OUTER)

        def slot_turn(p, value):
            distance = rows[pl.ds(128 + p, 1), :] + (
                spread[0] * rows[pl.ds(p, 1), :]
                + spread[1] * rows[pl.ds(32 + p, 1), :]
                + spread[2] * rows[pl.ds(64 + p, 1), :]
            )
            return value + lax.rsqrt(distance) * rows[pl.ds(96 + p, 1), :]

        checks = lax.fori_loop(0, 32, slot_turn, jnp.zeros((Q, 128), jnp.float32), unroll=4)
        stage[...] = dot(checks.T, fit_twice[...])
        for i in range(2):
            for pair in range(4):
                even = stage[pl.ds(64 * i + 2 * pair, 8, stride=8), :]
                odd = stage[pl.ds(64 * i + 2 * pair + 1, 8, stride=8), :]
                leaf[pair + 1, 2 * b + i + 2, 2:10, :] = jnp.where(half, even, odd)

    tables[0].wait()
    tables[1].wait()
    for b in range(4):
        upward(b)
    tables[2].wait()

    for c in range(4):
        for z in range(4):
            for x in range(4):
                piece = leaf[z + 1, 2 * x + c // 2 + 2, pl.ds(c % 2 + 2, 4, stride=2), :]
                lift_rows[16 * z + 4 * x : 16 * z + 4 * x + 4, 128 * c : 128 * c + 128] = piece
    stage[0:64] = dot(lift_rows[...], up[...])
    for pair in range(2):
        for x in range(4):
            even = stage[32 * pair + 4 * x : 32 * pair + 4 * x + 4, :]
            odd = stage[32 * pair + 16 + 4 * x : 32 * pair + 16 + 4 * x + 4, :]
            mid[pair + 1, x + 2, 2:6, :] = jnp.where(half, even, odd)
    for c in range(4):
        for z in range(2):
            for x in range(2):
                piece = mid[z + 1, 2 * x + c // 2 + 2, pl.ds(c % 2 + 2, 2, stride=2), :]
                lift_rows[4 * z + 2 * x : 4 * z + 2 * x + 2, 128 * c : 128 * c + 128] = piece
    stage[0:8] = dot(lift_rows[0:8], up[...])
    for x in range(2):
        even, odd = stage[2 * x : 2 * x + 2, :], stage[4 + 2 * x : 4 + 2 * x + 2, :]
        coarse[1, x + 2, 2:4, :] = jnp.where(half, even, odd)
    line = jnp.concatenate(
        [coarse[1, c // 2 + 2, c % 2 + 2 : c % 2 + 3, :] for c in range(4)], axis=1
    )
    tops_z[mz] = dot(jnp.broadcast_to(line, (8, 8 * Q)), up[...])

    pl.semaphore_wait(barrier, len(mates))
    shifts = [Shift("gz", 1 - 2 * s, s, pz_out.at[s], pz_in.at[s]) for s in range(2)]
    start(shifts)
    multi = [
        Shift("gz", 1, 6, leaf.at[4, pl.ds(2, 8)], leaf.at[0, pl.ds(2, 8)]),
        Shift("gz", -1, 7, leaf.at[1, pl.ds(2, 8)], leaf.at[5, pl.ds(2, 8)]),
        Shift("gz", 1, 8, mid.at[2, pl.ds(2, 4)], mid.at[0, pl.ds(2, 4)]),
        Shift("gz", -1, 9, mid.at[1, pl.ds(2, 4)], mid.at[3, pl.ds(2, 4)]),
        Shift("gz", 1, 10, coarse.at[1, pl.ds(2, 2)], coarse.at[0, pl.ds(2, 2)]),
        Shift("gz", -1, 11, coarse.at[1, pl.ds(2, 2)], coarse.at[2, pl.ds(2, 2)]),
    ]
    index = 20
    for step in range(1, nz):
        multi.append(Spread("gz", step, index, tops_z.at[mz]))
        index += 1
    start(multi)
    wait(shifts)

    @pl.when(mz > 0)
    def _():
        for x in range(8):
            cells[x + 1, pl.ds(16, 8, stride=16), :] = pz_in[0, 8 * x : 8 * x + 8, :]

    @pl.when(mz < nz - 1)
    def _():
        for x in range(8):
            cells[x + 1, pl.ds(16 + 9, 8, stride=16), :] = pz_in[1, 8 * x : 8 * x + 8, :]

    inner = pl.ds(1, 8)
    shifts = [
        Shift("gy", 1, 2, cells.at[inner, pl.ds(128, 16)], cells.at[inner, pl.ds(0, 16)]),
        Shift("gy", -1, 3, cells.at[inner, pl.ds(16, 16)], cells.at[inner, pl.ds(144, 16)]),
    ]
    start(shifts)
    wait(multi)
    for pair in range(nz // 2):
        even, odd = tops_z[2 * pair, 0:1, :], tops_z[2 * pair + 1, 0:1, :]
        tops_y[my, pair : pair + 1, :] = jnp.where(half, even, odd)
    packed = []
    for ref, tiles, width in ((leaf, 6, 8), (mid, 4, 4), (coarse, 3, 2)):
        for tile in range(tiles):
            for x in range(width):
                packed.append((ref, tile, x + 2, width))
    for number, (ref, tile, x, width) in enumerate(packed):
        my_out[0, 2 * number : 2 * number + 2, :] = ref[tile, x, width : width + 2, :]
        my_out[1, 2 * number : 2 * number + 2, :] = ref[tile, x, 2:4, :]
    multi = [Shift("gy", 1 - 2 * s, 12 + s, my_out.at[s], my_in.at[s]) for s in range(2)]
    for step in range(1, ny):
        multi.append(Spread("gy", step, index, tops_y.at[my]))
        index += 1
    start(multi)

    def put(target, pieces):
        turned = jnp.concatenate(pieces, axis=0).T
        sx, sy, sz = turned[0:32], turned[32:64], turned[64:96]
        target[0:96] = turned[0:96]
        target[96:128] = turned[96:128] * INV_FOUR_PI
        target[128:160] = (sx * sx + sy * sy) + sz * sz

    def column(x, y, oz):
        return cells[x, 16 * y + oz : 16 * y + oz + 8, :]

    def pair_turn(first, second, entry):
        for oz in range(3):
            put(planes.at[oz, entry], [column(x, y + 1, oz) for x in (first, second) for y in range(8)])

    def edge_turn(first, second, entry):
        for oz in range(3):
            pieces = []
            for x in (first, second):
                pieces += [column(x, 0, oz)] * 4 + [column(x, 9, oz)] * 4
            put(edges.at[oz, entry], pieces)

    def between(ref, low_entry, high_entry, entry):
        for oz in range(3):
            both = jnp.where(half, ref[oz, high_entry], ref[oz, low_entry])
            ref[oz, entry] = pltpu.roll(both, Q, 1)

    def pair_loop(k, carry):
        pair_turn(2 * k + 1, 2 * k + 2, 2 * k + 1)
        return carry

    def edge_loop(k, carry):
        edge_turn(2 * k + 1, 2 * k + 2, 2 * k + 1)
        return carry

    def between_loop(ref):
        def turn(k, carry):
            between(ref, 2 * k + 1, 2 * k + 3, 2 * k + 2)
            return carry

        lax.fori_loop(0, 3, turn, 0)

    group = lanes((8, 128)) // 32
    inside = lanes() % Q

    def spread_out(values, target, b):
        stage[...] = jnp.concatenate([values] * 4, axis=0).T
        for i in range(2):
            for block in range(2):
                result = None
                for z in range(4):
                    line = stage[pl.ds(64 * i + 4 * block + z, 8, stride=8), :]
                    result = line if z == 0 else jnp.where(group == z, line, result)
                target[2 * b + i, :, 128 * block : 128 * block + 128] = result

    def fill(target, move, oz, oy):
        entry = 2 * (move // 3) + move % 3
        if oy < 0:
            target[...] = jnp.where(inside < 8, edges[oz, entry], pltpu.roll(planes[oz, entry], 8, 1))
        else:
            target[...] = jnp.where(
                inside >= 56, edges[oz, entry], pltpu.roll(planes[oz, entry], 120, 1)
            )

    def add(source, move, oz, oy):
        b = move // 3
        dx = own_twice[b, 0:32] + 2.0 * (move % 3 - 1).astype(jnp.float32)
        dy = own_twice[b, 32:64] + 2.0 * oy
        dz = own_twice[b, 64:96] + 2.0 * (oz - 1).astype(jnp.float32)
        squared = 0.25 * (dx * dx + dy * dy + dz * dz) + SOFTEN_SQUARED

        def source_turn(p, value):
            distance = (squared + source[pl.ds(128 + p, 1), :]) + (
                dx * source[pl.ds(p, 1), :]
                + dy * source[pl.ds(32 + p, 1), :]
                + dz * source[pl.ds(64 + p, 1), :]
            )
            return value + lax.rsqrt(distance) * source[pl.ds(96 + p, 1), :]

        near_sum[b] = lax.fori_loop(0, 32, source_turn, near_sum[b], unroll=32)

    def add_straight(move, oz):
        add(planes.at[oz, 2 * (move // 3) + move % 3], move, oz, 0)

    near_sum[...] = jnp.zeros_like(near_sum)
    lax.fori_loop(0, 4, pair_loop, 0)
    between_loop(planes)

    def straight_turn(number, carry):
        add_straight(number // 3 + 1, number % 3)
        return carry

    lax.fori_loop(0, 30, straight_turn, 0)

    wait(shifts)
    shifts = [
        Shift("gx", 1, 4, cells.at[8], cells.at[0]),
        Shift("gx", -1, 5, cells.at[1], cells.at[9]),
    ]
    start(shifts)
    wait(multi)
    for y in range(ny):
        tops[mx, y * (nz // 2) : (y + 1) * (nz // 2), :] = tops_y[y, 0 : nz // 2, :]

    @pl.when(my > 0)
    def _():
        for number, (ref, tile, x, width) in enumerate(packed):
            ref[tile, x, 0:2, :] = my_in[0, 2 * number : 2 * number + 2, :]

    @pl.when(my < ny - 1)
    def _():
        for number, (ref, tile, x, width) in enumerate(packed):
            ref[tile, x, width + 2 : width + 4, :] = my_in[1, 2 * number : 2 * number + 2, :]

    multi = []
    for number, (ref, tiles, width) in enumerate(((leaf, 6, 8), (mid, 4, 4), (coarse, 3, 2))):
        every = pl.ds(0, tiles)
        left, right = ref.at[every, pl.ds(0, 2)], ref.at[every, pl.ds(width + 2, 2)]
        multi.append(Shift("gx", 1, 14 + 2 * number, ref.at[every, pl.ds(width, 2)], left))
        multi.append(Shift("gx", -1, 15 + 2 * number, ref.at[every, pl.ds(2, 2)], right))
    for step in range(1, nx):
        multi.append(Spread("gx", step, index, tops.at[mx]))
        index += 1
    start(multi)

    lax.fori_loop(0, 4, edge_loop, 0)
    between_loop(edges)

    def fill_both(slabs, number):
        for slab, oy in zip(slabs, (-1, 1)):
            fill(slab, number // 3 + 1, number % 3, oy)

    def add_both(slabs, number):
        for slab, oy in zip(slabs, (-1, 1)):
            add(slab, number // 3 + 1, number % 3, oy)

    first_slabs, second_slabs = (slab0, slab1), (slab2, slab3)
    fill_both(first_slabs, 0)

    def shifted_turn(number, carry):
        fill_both(second_slabs, 2 * number + 1)
        add_both(first_slabs, 2 * number)
        fill_both(first_slabs, jnp.minimum(2 * number + 2, 29))
        add_both(second_slabs, 2 * number + 1)
        return carry

    lax.fori_loop(0, 15, shifted_turn, 0)

    wait(shifts)
    for turn, ref in ((pair_turn, planes), (edge_turn, edges)):
        turn(9, 0, 9)
        between(ref, 9, 1, 0)
        between(ref, 7, 9, 8)

    def outer_turn(number, carry):
        move, oz = 11 * (number // 3), number % 3
        for slab, oy in zip(first_slabs, (-1, 1)):
            fill(slab, move, oz, oy)
        add_straight(move, oz)
        for slab, oy in zip(first_slabs, (-1, 1)):
            add(slab, move, oz, oy)
        return carry

    lax.fori_loop(0, 6, outer_turn, 0)
    for b in range(4):
        spread_out(near_sum[b], near_out, b)
    wait(multi)
    for table in tables[3:]:
        table.wait()

    def far_turn(number, value):
        sx = number // (ny * (nz // 2))
        sy = number // (nz // 2) % ny
        sz = 2 * (number % (nz // 2))
        row = tops[sx, pl.ds(number % (ny * (nz // 2)), 1), :]
        dx = (mx - sx).astype(jnp.float32)
        dy = (my - sy).astype(jnp.float32)
        dz = (mz - sz).astype(jnp.float32) - jnp.where(half, 0.0, 1.0)
        first, second, third = base[0] + dx, base[1] + dy, base[2] + dz
        squared = first * first + second * second + third * third
        reach = jnp.maximum(jnp.maximum(jnp.abs(dx), jnp.abs(dy)), jnp.abs(dz))
        weight = jnp.where(reach >= 2.0, row * INV_FOUR_PI, 0.0)
        kernel = jnp.where(reach >= 2.0, lax.rsqrt(squared), 0.0)
        return value + kernel * weight

    checks = lax.fori_loop(0, nx * ny * (nz // 2), far_turn, jnp.zeros((Q, 128), jnp.float32))
    top_local = jnp.sum(dot(checks.T, fit[...]), axis=0, keepdims=True)

    def split(values):
        first = values.astype(jnp.bfloat16)
        return first, (values - first.astype(jnp.float32)).astype(jnp.bfloat16)

    def wide_turn(ux, carry):
        for uy in range(8):
            for tile in range(6):
                for gx in range(2):
                    piece = leaf[tile, ux + 4 * gx, pl.ds(uy, 2, stride=4), :]
                    gather[uy, 4 * tile + 2 * gx : 4 * tile + 2 * gx + 2, :] = piece
        for uy in range(8):
            for t in range(3):
                first, second = split(gather[uy, 4 * t : 4 * t + 16, :])
                wide[0, ux, uy, :, 128 * t : 128 * t + 128] = first
                wide[1, ux, uy, :, 128 * t : 128 * t + 128] = second
        return carry

    lax.fori_loop(0, 8, wide_turn, 0)

    def narrow_turn(sx, carry):
        for sy in range(6):
            for tile in range(4):
                for gx in range(2):
                    piece = mid[tile, sx + 2 * gx, pl.ds(sy, 2, stride=2), :]
                    gather_mid[sy, 4 * tile + 2 * gx : 4 * tile + 2 * gx + 2, :] = piece
        for sy in range(6):
            for t in range(3):
                last = jnp.broadcast_to(coarse[t, sx, sy : sy + 1, :], (8, 128))
                both = jnp.concatenate([gather_mid[sy, 4 * t : 4 * t + 8, :], last], axis=0)
                first, second = split(both)
                narrow[0, sx, sy, :, 128 * t : 128 * t + 128] = first
                narrow[1, sx, sy, :, 128 * t : 128 * t + 128] = second
        return carry

    lax.fori_loop(0, 6, narrow_turn, 0)
    total[...] = jnp.zeros_like(total)

    def list_turn(number, carry):
        sx = number // 3
        lefts, highs, lows = [], [], []
        for k in range(2):
            sy = 2 * (number % 3) + k
            columns = []
            for h in range(2):
                columns += [wide[h, sx + 2 * (c // 2), sy + 2 * (c % 2)] for c in range(4)]
                columns.append(narrow[h, sx, sy])
            lefts.append(jnp.concatenate(columns, axis=0))
            places = [(sx + 1 - c // 2, sy + 1 - c % 2) for c in range(4)]
            highs.append(jnp.concatenate([high[a, b] for a, b in places], axis=1))
            lows.append(jnp.concatenate([low[a, b] for a, b in places], axis=1))
        left = jnp.concatenate(lefts, axis=1)
        right_high = jnp.concatenate(highs, axis=0)
        right_low = jnp.concatenate(lows, axis=0)
        first = jnp.dot(left, right_high, preferred_element_type=jnp.float32)
        second = jnp.dot(left[:80], right_low, preferred_element_type=jnp.float32)
        total[...] += first[:80] + first[80:] + second
        return carry

    lax.fori_loop(0, 18, list_turn, 0)
    fitted = jnp.concatenate(
        [dot(total[:, 128 * pair : 128 * pair + 128], pair_fit[...]) for pair in range(4)], axis=1
    )
    line = fitted[72:80] + dot(jnp.broadcast_to(top_local, (8, Q)), down[...])
    order = [2 * c + z for z in range(2) for c in range(4)]
    boxes = jnp.concatenate([line[0:1, Q * c : Q * c + Q] for c in order], axis=0)
    boxes = fitted[64:72] + dot(boxes, down[...])
    for c in range(4):
        for z in range(4):
            column = Q * (2 * c + z % 2)
            stage[16 * c + 4 * z : 16 * c + 4 * z + 4, 0:Q] = boxes[
                4 * (z // 2) : 4 * (z // 2) + 4, column : column + Q
            ]
    lines = fitted[0:64] + dot(stage[0:64, 0:Q], down[...])
    for h in range(4):
        local[h] = lines[:, 128 * h : 128 * h + 128]

    even = lanes() % 2 == 0
    for b in range(4):
        for h in range(4):
            for cy in range(2):
                for gy in range(2):
                    start_row = 16 * (2 * (b % 2) + cy) + 2 * (b // 2) + gy
                    piece = local[h, pl.ds(start_row, 4, stride=4), :]
                    target = 64 * (h // 2) + 8 * (2 * (cy + 2 * gy) + h % 2)
                    stage[pl.ds(target, 4, stride=2), :] = piece
                    stage[pl.ds(target + 1, 4, stride=2), :] = piece
        turned = stage[...].T * INV_FOUR_PI
        rows[0:Q] = jnp.where(even, turned[0:Q], turned[Q : 2 * Q])
        position = own[b]
        tx, ty, tz = -2.0 * position[0:32], -2.0 * position[32:64], -2.0 * position[64:96]
        squared = 0.25 * (tx * tx + ty * ty + tz * tz) + OUTER * OUTER

        def point_turn(k, value):
            distance = squared + (
                tx * spread[0, pl.ds(k, 1), :]
                + ty * spread[1, pl.ds(k, 1), :]
                + tz * spread[2, pl.ds(k, 1), :]
            )
            return value + lax.rsqrt(distance) * rows[pl.ds(k, 1), :]

        value = lax.fori_loop(0, Q, point_turn, near_sum[b], unroll=16)
        spread_out(value, potential, b)


def per_device(particles, counts):
    spread, fit_twice, up, base, fit, pair_fit, down, high, low = constant_tables()
    sizes = tuple(lax.axis_size(axis) for axis in AXES)
    nx, ny, nz = sizes
    copies = 20 + sum(sizes) - 3
    vmem = pl.BlockSpec(memory_space=pltpu.VMEM)
    remote = pl.BlockSpec(memory_space=pl.ANY)
    single = jnp.float32

    def array(*shape):
        return pltpu.VMEM(shape, single)

    return pl.pallas_call(
        functools.partial(fused_kernel, sizes),
        out_shape=(jax.ShapeDtypeStruct((8, 8, 256), single),) * 2,
        in_specs=[vmem] * 2 + [remote] * 9,
        out_specs=(vmem, vmem),
        scratch_shapes=[
            array(*spread.shape),
            array(*fit_twice.shape),
            array(*up.shape),
            array(*base.shape),
            array(*fit.shape),
            array(*pair_fit.shape),
            array(*down.shape),
            array(10, 160, 128),
            array(3, 10, 160, 128),
            array(3, 10, 160, 128),
            array(4, 128, 128),
            array(4, 96, 128),
            array(160, 128),
            array(160, 128),
            array(160, 128),
            array(160, 128),
            array(160, 128),
            array(6, 12, 16, 128),
            array(4, 8, 8, 128),
            array(3, 6, 8, 128),
            array(nz, 8, 128),
            array(ny, -(-nz // 16) * 8, 128),
            array(nx, -(-ny * nz // 16) * 8, 128),
            array(128, 128),
            array(64, 512),
            array(2, 64, 128),
            array(2, 64, 128),
            array(2, 144, 128),
            array(2, 144, 128),
            array(8, 24, 128),
            array(6, 16, 128),
            pltpu.VMEM((2, 8, 8, 16, 384), jnp.bfloat16),
            pltpu.VMEM((2, 6, 6, 16, 384), jnp.bfloat16),
            array(80, 512),
            array(4, 32, 128),
            array(4, 64, 128),
            pltpu.VMEM(high.shape, jnp.bfloat16),
            pltpu.VMEM(low.shape, jnp.bfloat16),
            pltpu.SemaphoreType.DMA((copies,)),
            pltpu.SemaphoreType.DMA((copies,)),
            pltpu.SemaphoreType.DMA((9,)),
        ],
        compiler_params=pltpu.CompilerParams(
            collective_id=0, has_side_effects=True, vmem_limit_bytes=56 << 20
        ),
        cost_estimate=pl.CostEstimate(flops=8 << 30, bytes_accessed=12 << 20, transcendentals=0),
    )(particles, counts, spread, fit_twice, up, base, fit, pair_fit, down, high, low)


def solution(mesh):
    placed = (P("gx", "gy", "gz", None), P("gx", "gy", "gz"))
    return jax.shard_map(
        per_device,
        mesh=mesh,
        in_specs=placed,
        out_specs=(P("gx", "gy", "gz"), P("gx", "gy", "gz")),
        check_vma=False,
    )
```

```python
import functools
import math

import jax
import jax.numpy as jnp
import ml_dtypes
import numpy as np
from jax import lax
from jax.experimental import pallas as pl
from jax.experimental.pallas import tpu as pltpu
from jax.sharding import PartitionSpec as P

Q = 64
INV_FOUR_PI = 0.07957747154594767
INNER = 0.9
OUTER = 1.5
PARENT_CHECK = 3.0
SOFTEN_SQUARED = 0.0625
REGULAR = 0.01
HIGHEST = lax.Precision.HIGHEST
MESH = pl.DeviceIdType.MESH
AXES = ("gx", "gy", "gz")


def sphere(number):
    order = np.arange(number, dtype=np.float64)
    height = 1.0 - (2.0 * order + 1.0) / number
    radial = np.sqrt(1.0 - height * height)
    turning = order * (math.pi * (3.0 - math.sqrt(5.0)))
    return np.stack([radial * np.cos(turning), radial * np.sin(turning), height])


def green(vectors):
    return INV_FOUR_PI / np.sqrt(np.sum(vectors * vectors, axis=0))


def constant_tables():
    points = sphere(Q)
    kernel = green(OUTER * points[:, :, None] - INNER * points[:, None, :])
    normal = kernel.T @ kernel
    normal = normal + REGULAR * np.trace(normal) / Q * np.eye(Q)
    lower = np.linalg.cholesky(normal)
    fit = np.linalg.solve(lower, kernel.T) / np.diag(lower)[:, None]
    up = np.zeros((8 * Q, Q))
    down = np.zeros((Q, 8 * Q))
    for child in range(8):
        offset = np.array([child // 4, child // 2 % 2, child % 2]) - 0.5
        vectors = PARENT_CHECK * points[:, :, None] - INNER * points[:, None, :]
        upper = green(vectors - offset[:, None, None])
        up[child * Q : (child + 1) * Q] = (2.0 * fit @ upper).T
        vectors = INNER * points[:, :, None] - PARENT_CHECK * points[:, None, :]
        lower = green(vectors + offset[:, None, None])
        down[:, child * Q : (child + 1) * Q] = lower.T @ fit
    base = INNER * (points[:, :, None] - points[:, None, :])
    table = np.zeros((7, 7, 6, Q, 2, Q), np.float32)
    for ox in range(-3, 4):
        for oy in range(-3, 4):
            for sz in range(6):
                for cz in range(2):
                    offset = np.array([ox, oy, sz - 2 - cz], np.float64)
                    if np.max(np.abs(offset)) >= 2:
                        values = green(base - offset[:, None, None])
                        table[ox + 3, oy + 3, sz, :, cz, :] = values.T
    table = table.reshape(7, 7, 6 * Q, 2 * Q)
    high = table.astype(ml_dtypes.bfloat16)
    low = (table - high.astype(np.float32)).astype(ml_dtypes.bfloat16)
    spread = np.repeat((OUTER * points)[:, :, None], 128, axis=2)
    single = np.float32
    return (
        spread.astype(single),
        np.tile(fit.T, (1, 2)).astype(single),
        np.tile(up, (1, 2)).astype(single),
        np.tile(base, (1, 1, 2)).astype(single),
        fit.astype(single),
        np.kron(np.eye(2), fit).astype(single),
        down.astype(single),
        high,
        low,
    )


def dot(left, right):
    return jnp.dot(left, right, precision=HIGHEST, preferred_element_type=jnp.float32)


def lanes(shape=(1, 128)):
    return lax.broadcasted_iota(jnp.int32, shape, 1)


def fused_kernel(
    sizes,
    part,
    counts,
    spread_far,
    fit_twice_far,
    up_far,
    base_far,
    fit_far,
    pair_fit_far,
    down_far,
    high_far,
    low_far,
    potential,
    near_out,
    spread,
    fit_twice,
    up,
    base,
    fit,
    pair_fit,
    down,
    cells,
    planes,
    edges,
    own,
    own_twice,
    rows,
    slab0,
    slab1,
    slab2,
    slab3,
    leaf,
    mid,
    coarse,
    tops_z,
    tops_y,
    tops,
    stage,
    lift_rows,
    pz_out,
    pz_in,
    my_out,
    my_in,
    gather,
    gather_mid,
    wide,
    narrow,
    total,
    near_sum,
    local,
    high,
    low,
    send_sem,
    recv_sem,
    table_sem,
):
    nx, ny, nz = sizes
    place = {axis: lax.axis_index(axis) for axis in AXES}
    count = dict(zip(AXES, sizes))
    mx, my, mz = (place[axis] for axis in AXES)
    half = lanes() < Q

    pairs = (
        (spread_far, spread),
        (fit_twice_far, fit_twice),
        (up_far, up),
        (base_far, base),
        (fit_far, fit),
        (pair_fit_far, pair_fit),
        (down_far, down),
        (high_far, high),
        (low_far, low),
    )
    tables = [
        pltpu.make_async_copy(far, here, table_sem.at[number])
        for number, (far, here) in enumerate(pairs)
    ]
    for table in tables:
        table.start()

    def clear(ref):
        def turn(number, carry):
            ref[number] = jnp.zeros(ref.shape[1:], jnp.float32)
            return carry

        lax.fori_loop(0, ref.shape[0], turn, 0)

    for ref in (cells, leaf, mid, coarse, my_out, tops_y, tops):
        clear(ref)

    barrier = pltpu.get_barrier_semaphore()
    mates = [
        (axis, lax.rem(place[axis] + step, count[axis]))
        for axis in AXES
        for step in range(1, count[axis])
    ]
    for axis, mate in mates:
        pl.semaphore_signal(barrier, inc=1, device_id={axis: mate}, device_id_type=MESH)

    class Shift:
        def __init__(self, axis, step, index, source, target):
            m, n = place[axis], count[axis]
            first, last = m > 0, m < n - 1
            self.sends, self.receives = (last, first) if step == 1 else (first, last)
            self.copy = pltpu.make_async_remote_copy(
                src_ref=source,
                dst_ref=target,
                send_sem=send_sem.at[index],
                recv_sem=recv_sem.at[index],
                device_id={axis: lax.rem(m + step + n, n)},
                device_id_type=MESH,
            )

        def start(self):
            pl.when(self.sends)(lambda: self.copy.start())

        def wait(self):
            pl.when(self.sends)(lambda: self.copy.wait_send())
            pl.when(self.receives)(lambda: self.copy.wait_recv())

    class Spread:
        def __init__(self, axis, step, index, block):
            m, n = place[axis], count[axis]
            self.copy = pltpu.make_async_remote_copy(
                src_ref=block,
                dst_ref=block,
                send_sem=send_sem.at[index],
                recv_sem=recv_sem.at[index],
                device_id={axis: lax.rem(m + step, n)},
                device_id_type=MESH,
            )

        def start(self):
            self.copy.start()

        def wait(self):
            self.copy.wait_send()
            self.copy.wait_recv()

    def start(copies):
        for copy in copies:
            copy.start()

    def wait(copies):
        for copy in copies:
            copy.wait()

    slot = lanes((8, 128)) - 96
    square = lax.broadcasted_iota(jnp.int32, (8, 8), 0) == lax.broadcasted_iota(jnp.int32, (8, 8), 1)

    def mask_turn(x, carry):
        present = counts[x].astype(jnp.float32)
        for y in range(8):
            line = jnp.where(square, jnp.broadcast_to(present[y : y + 1], (8, 8)), 0.0)
            number = jnp.sum(line, axis=1, keepdims=True)
            values = jnp.where(slot.astype(jnp.float32) < number, part[x, y], 0.0)
            cells[x + 1, 16 * (y + 1) + 1 : 16 * (y + 1) + 9, :] = values
        return carry

    lax.fori_loop(0, 8, mask_turn, 0)
    for x in range(8):
        for side, z in ((0, 8), (1, 1)):
            pz_out[side, 8 * x : 8 * x + 8, :] = cells[x + 1, pl.ds(16 + z, 8, stride=16), :]

    def upward(b):
        pieces = [
            cells[2 * b + 1 + i, 16 * (y + 1) + 1 : 16 * (y + 1) + 9, :]
            for i in range(2)
            for y in range(8)
        ]
        turned = jnp.concatenate(pieces, axis=0).T
        own[b] = turned
        own_twice[b] = -2.0 * turned[0:96]
        tx, ty, tz = turned[0:32], turned[32:64], turned[64:96]
        rows[0:96] = -2.0 * turned[0:96]
        rows[96:128] = turned[96:128] * INV_FOUR_PI
        rows[128:160] = (tx * tx + ty * ty) + (tz * tz + OUTER * OUTER)

        def slot_turn(p, value):
            distance = rows[pl.ds(128 + p, 1), :] + (
                spread[0] * rows[pl.ds(p, 1), :]
                + spread[1] * rows[pl.ds(32 + p, 1), :]
                + spread[2] * rows[pl.ds(64 + p, 1), :]
            )
            return value + lax.rsqrt(distance) * rows[pl.ds(96 + p, 1), :]

        checks = lax.fori_loop(0, 32, slot_turn, jnp.zeros((Q, 128), jnp.float32), unroll=4)
        stage[...] = dot(checks.T, fit_twice[...])
        for i in range(2):
            for pair in range(4):
                even = stage[pl.ds(64 * i + 2 * pair, 8, stride=8), :]
                odd = stage[pl.ds(64 * i + 2 * pair + 1, 8, stride=8), :]
                leaf[pair + 1, 2 * b + i + 2, 2:10, :] = jnp.where(half, even, odd)

    tables[0].wait()
    tables[1].wait()
    for b in range(4):
        upward(b)
    tables[2].wait()

    for c in range(4):
        for z in range(4):
            for x in range(4):
                piece = leaf[z + 1, 2 * x + c // 2 + 2, pl.ds(c % 2 + 2, 4, stride=2), :]
                lift_rows[16 * z + 4 * x : 16 * z + 4 * x + 4, 128 * c : 128 * c + 128] = piece
    stage[0:64] = dot(lift_rows[...], up[...])
    for pair in range(2):
        for x in range(4):
            even = stage[32 * pair + 4 * x : 32 * pair + 4 * x + 4, :]
            odd = stage[32 * pair + 16 + 4 * x : 32 * pair + 16 + 4 * x + 4, :]
            mid[pair + 1, x + 2, 2:6, :] = jnp.where(half, even, odd)
    for c in range(4):
        for z in range(2):
            for x in range(2):
                piece = mid[z + 1, 2 * x + c // 2 + 2, pl.ds(c % 2 + 2, 2, stride=2), :]
                lift_rows[4 * z + 2 * x : 4 * z + 2 * x + 2, 128 * c : 128 * c + 128] = piece
    stage[0:8] = dot(lift_rows[0:8], up[...])
    for x in range(2):
        even, odd = stage[2 * x : 2 * x + 2, :], stage[4 + 2 * x : 4 + 2 * x + 2, :]
        coarse[1, x + 2, 2:4, :] = jnp.where(half, even, odd)
    line = jnp.concatenate(
        [coarse[1, c // 2 + 2, c % 2 + 2 : c % 2 + 3, :] for c in range(4)], axis=1
    )
    tops_z[mz] = dot(jnp.broadcast_to(line, (8, 8 * Q)), up[...])

    pl.semaphore_wait(barrier, len(mates))
    multi = [
        Shift("gz", 1, 6, leaf.at[4, pl.ds(2, 8)], leaf.at[0, pl.ds(2, 8)]),
        Shift("gz", -1, 7, leaf.at[1, pl.ds(2, 8)], leaf.at[5, pl.ds(2, 8)]),
        Shift("gz", 1, 8, mid.at[2, pl.ds(2, 4)], mid.at[0, pl.ds(2, 4)]),
        Shift("gz", -1, 9, mid.at[1, pl.ds(2, 4)], mid.at[3, pl.ds(2, 4)]),
        Shift("gz", 1, 10, coarse.at[1, pl.ds(2, 2)], coarse.at[0, pl.ds(2, 2)]),
        Shift("gz", -1, 11, coarse.at[1, pl.ds(2, 2)], coarse.at[2, pl.ds(2, 2)]),
    ]
    index = 20
    for step in range(1, nz):
        multi.append(Spread("gz", step, index, tops_z.at[mz]))
        index += 1
    start(multi)
    shifts = [Shift("gz", 1 - 2 * s, s, pz_out.at[s], pz_in.at[s]) for s in range(2)]
    start(shifts)
    wait(multi)
    for pair in range(nz // 2):
        even, odd = tops_z[2 * pair, 0:1, :], tops_z[2 * pair + 1, 0:1, :]
        tops_y[my, pair : pair + 1, :] = jnp.where(half, even, odd)
    packed = []
    for ref, tiles, width in ((leaf, 6, 8), (mid, 4, 4), (coarse, 3, 2)):
        for tile in range(tiles):
            for x in range(width):
                packed.append((ref, tile, x + 2, width))
    for number, (ref, tile, x, width) in enumerate(packed):
        my_out[0, 2 * number : 2 * number + 2, :] = ref[tile, x, width : width + 2, :]
        my_out[1, 2 * number : 2 * number + 2, :] = ref[tile, x, 2:4, :]
    multi = [Shift("gy", 1 - 2 * s, 12 + s, my_out.at[s], my_in.at[s]) for s in range(2)]
    for step in range(1, ny):
        multi.append(Spread("gy", step, index, tops_y.at[my]))
        index += 1
    start(multi)

    wait(shifts)

    @pl.when(mz > 0)
    def _():
        for x in range(8):
            cells[x + 1, pl.ds(16, 8, stride=16), :] = pz_in[0, 8 * x : 8 * x + 8, :]

    @pl.when(mz < nz - 1)
    def _():
        for x in range(8):
            cells[x + 1, pl.ds(16 + 9, 8, stride=16), :] = pz_in[1, 8 * x : 8 * x + 8, :]

    inner = pl.ds(1, 8)
    shifts = [
        Shift("gy", 1, 2, cells.at[inner, pl.ds(128, 16)], cells.at[inner, pl.ds(0, 16)]),
        Shift("gy", -1, 3, cells.at[inner, pl.ds(16, 16)], cells.at[inner, pl.ds(144, 16)]),
    ]
    start(shifts)
    def put(target, pieces):
        turned = jnp.concatenate(pieces, axis=0).T
        sx, sy, sz = turned[0:32], turned[32:64], turned[64:96]
        target[0:128] = turned
        target[128:160] = (sx * sx + sy * sy) + sz * sz

    def column(x, y, oz):
        return cells[x, 16 * y + oz : 16 * y + oz + 8, :]

    def pair_turn(first, second, entry):
        for oz in range(3):
            put(planes.at[oz, entry], [column(x, y + 1, oz) for x in (first, second) for y in range(8)])

    def edge_turn(first, second, entry):
        for oz in range(3):
            pieces = []
            for x in (first, second):
                pieces += [column(x, 0, oz)] * 4 + [column(x, 9, oz)] * 4
            put(edges.at[oz, entry], pieces)

    def between(ref, low_entry, high_entry, entry):
        for oz in range(3):
            both = jnp.where(half, ref[oz, high_entry], ref[oz, low_entry])
            ref[oz, entry] = pltpu.roll(both, Q, 1)

    def pair_loop(k, carry):
        pair_turn(2 * k + 1, 2 * k + 2, 2 * k + 1)
        return carry

    def edge_loop(k, carry):
        edge_turn(2 * k + 1, 2 * k + 2, 2 * k + 1)
        return carry

    def between_loop(ref):
        def turn(k, carry):
            between(ref, 2 * k + 1, 2 * k + 3, 2 * k + 2)
            return carry

        lax.fori_loop(0, 3, turn, 0)

    group = lanes((8, 128)) // 32
    inside = lanes() % Q

    def spread_out(values, target, b):
        stage[...] = jnp.concatenate([values] * 4, axis=0).T
        for i in range(2):
            for block in range(2):
                result = None
                for z in range(4):
                    line = stage[pl.ds(64 * i + 4 * block + z, 8, stride=8), :]
                    result = line if z == 0 else jnp.where(group == z, line, result)
                target[2 * b + i, :, 128 * block : 128 * block + 128] = result

    def fill(target, entry, oz, oy):
        if oy < 0:
            target[...] = jnp.where(inside < 8, edges[oz, entry], pltpu.roll(planes[oz, entry], 8, 1))
        else:
            target[...] = jnp.where(
                inside >= 56, edges[oz, entry], pltpu.roll(planes[oz, entry], 120, 1)
            )

    def add(source, moves, oz, oy):
        sides = []
        dz = 2.0 * (oz - 1).astype(jnp.float32)
        for b, ox in moves:
            x = own_twice[b, 0:32] + 2.0 * ox
            y = own_twice[b, 32:64] + 2.0 * oy
            z = own_twice[b, 64:96] + dz
            sides.append((x, y, z, 0.25 * (x * x + y * y + z * z) + SOFTEN_SQUARED))

        def source_turn(p, values):
            sx, sy, sz = (source[pl.ds(32 * c + p, 1), :] for c in range(3))
            strength, length = source[pl.ds(96 + p, 1), :], source[pl.ds(128 + p, 1), :]
            result = []
            for (x, y, z, squared), value in zip(sides, values):
                distance = (squared + length) + (x * sx + y * sy + z * sz)
                result.append(value + lax.rsqrt(distance) * strength)
            return tuple(result)

        zero = jnp.zeros((32, 128), jnp.float32)
        values = lax.fori_loop(0, 32, source_turn, (zero,) * len(moves), unroll=32)
        for (b, ox), value in zip(moves, values):
            near_sum[b] += value

    def single_moves(k):
        return 2 * k + 1, [(k, 0.0)]

    def double_moves(k):
        return 2 * k + 2, [(k + 1, -1.0), (k, 1.0)]

    near_sum[...] = jnp.zeros_like(near_sum)
    lax.fori_loop(0, 4, pair_loop, 0)
    between_loop(planes)

    def straight_turn(number, carry):
        for oz in range(3):
            for entry, moves in (single_moves(number), double_moves(number)):
                add(planes.at[oz, entry], moves, jnp.int32(oz), 0)
        return carry

    lax.fori_loop(0, 1, straight_turn, 0)
    wait(multi)
    for y in range(ny):
        tops[mx, y * (nz // 2) : (y + 1) * (nz // 2), :] = tops_y[y, 0 : nz // 2, :]

    @pl.when(my > 0)
    def _():
        for number, (ref, tile, x, width) in enumerate(packed):
            ref[tile, x, 0:2, :] = my_in[0, 2 * number : 2 * number + 2, :]

    @pl.when(my < ny - 1)
    def _():
        for number, (ref, tile, x, width) in enumerate(packed):
            ref[tile, x, width + 2 : width + 4, :] = my_in[1, 2 * number : 2 * number + 2, :]

    multi = []
    for number, (ref, tiles, width) in enumerate(((leaf, 6, 8), (mid, 4, 4), (coarse, 3, 2))):
        every = pl.ds(0, tiles)
        left, right = ref.at[every, pl.ds(0, 2)], ref.at[every, pl.ds(width + 2, 2)]
        multi.append(Shift("gx", 1, 14 + 2 * number, ref.at[every, pl.ds(width, 2)], left))
        multi.append(Shift("gx", -1, 15 + 2 * number, ref.at[every, pl.ds(2, 2)], right))
    for step in range(1, nx):
        multi.append(Spread("gx", step, index, tops.at[mx]))
        index += 1
    start(multi)
    lax.fori_loop(1, 3, straight_turn, 0)
    for oz in range(3):
        add(planes.at[oz, 7], [(3, 0.0)], jnp.int32(oz), 0)

    wait(shifts)
    shifts = [
        Shift("gx", 1, 4, cells.at[8], cells.at[0]),
        Shift("gx", -1, 5, cells.at[1], cells.at[9]),
    ]
    start(shifts)
    lax.fori_loop(0, 4, edge_loop, 0)
    between_loop(edges)

    def shifted(parts, oz):
        slabs = iter((slab0, slab1, slab2, slab3))
        jobs = [(next(slabs), entry, moves, oy) for entry, moves in parts for oy in (-1, 1)]
        for slab, entry, moves, oy in jobs:
            fill(slab, entry, oz, oy)
        for slab, entry, moves, oy in jobs:
            add(slab, moves, oz, oy)

    def shifted_turn(number, carry):
        k = number // 3
        shifted([single_moves(k), double_moves(k)], number % 3)
        return carry

    lax.fori_loop(0, 6, shifted_turn, 0)
    wait(multi)
    for table in tables[3:]:
        table.wait()

    def split(values):
        first = values.astype(jnp.bfloat16)
        return first, (values - first.astype(jnp.float32)).astype(jnp.bfloat16)

    def wide_turn(ux, carry):
        for uy in range(8):
            for tile in range(6):
                for gx in range(2):
                    piece = leaf[tile, ux + 4 * gx, pl.ds(uy, 2, stride=4), :]
                    gather[uy, 4 * tile + 2 * gx : 4 * tile + 2 * gx + 2, :] = piece
        for uy in range(8):
            for t in range(3):
                first, second = split(gather[uy, 4 * t : 4 * t + 16, :])
                wide[0, ux, uy, :, 128 * t : 128 * t + 128] = first
                wide[1, ux, uy, :, 128 * t : 128 * t + 128] = second
        return carry

    lax.fori_loop(0, 8, wide_turn, 0)

    def narrow_turn(sx, carry):
        for sy in range(6):
            for tile in range(4):
                for gx in range(2):
                    piece = mid[tile, sx + 2 * gx, pl.ds(sy, 2, stride=2), :]
                    gather_mid[sy, 4 * tile + 2 * gx : 4 * tile + 2 * gx + 2, :] = piece
        for sy in range(6):
            for t in range(3):
                last = jnp.broadcast_to(coarse[t, sx, sy : sy + 1, :], (8, 128))
                both = jnp.concatenate([gather_mid[sy, 4 * t : 4 * t + 8, :], last], axis=0)
                first, second = split(both)
                narrow[0, sx, sy, :, 128 * t : 128 * t + 128] = first
                narrow[1, sx, sy, :, 128 * t : 128 * t + 128] = second
        return carry

    lax.fori_loop(0, 6, narrow_turn, 0)
    total[...] = jnp.zeros_like(total)

    def list_part(number):
        sx = number // 3
        lefts, highs, lows = [], [], []
        for k in range(2):
            sy = 2 * (number % 3) + k
            columns = []
            for h in range(2):
                columns += [wide[h, sx + 2 * (c // 2), sy + 2 * (c % 2)] for c in range(4)]
                columns.append(narrow[h, sx, sy])
            lefts.append(jnp.concatenate(columns, axis=0))
            places = [(sx + 1 - c // 2, sy + 1 - c % 2) for c in range(4)]
            highs.append(jnp.concatenate([high[a, b] for a, b in places], axis=1))
            lows.append(jnp.concatenate([low[a, b] for a, b in places], axis=1))
        left = jnp.concatenate(lefts, axis=1)
        right_high = jnp.concatenate(highs, axis=0)
        right_low = jnp.concatenate(lows, axis=0)
        first = jnp.dot(left, right_high, preferred_element_type=jnp.float32)
        second = jnp.dot(left[:80], right_low, preferred_element_type=jnp.float32)
        total[...] += first[:80] + first[80:] + second

    def mixed_turn(number, carry):
        list_part(2 * number)
        list_part(2 * number + 1)
        return shifted_turn(number + 6, carry)

    lax.fori_loop(0, 3, mixed_turn, 0)

    def last_turn(oz, carry):
        list_part(2 * oz + 6)
        list_part(2 * oz + 7)
        shifted([single_moves(3)], oz)
        return carry

    lax.fori_loop(0, 3, last_turn, 0)

    wait(shifts)
    for turn, ref in ((pair_turn, planes), (edge_turn, edges)):
        turn(9, 0, 9)
        between(ref, 9, 1, 0)
        between(ref, 7, 9, 8)

    def outer_turn(oz, carry):
        for k, part in enumerate(((0, [(0, -1.0)]), (8, [(3, 1.0)]))):
            list_part(2 * oz + 12 + k)
            entry, moves = part
            add(planes.at[oz, entry], moves, oz, 0)
            shifted([part], oz)
        return carry

    lax.fori_loop(0, 3, outer_turn, 0)
    for b in range(4):
        spread_out(near_sum[b], near_out, b)

    def far_turn(number, value):
        sx = number // (ny * (nz // 2))
        sy = number // (nz // 2) % ny
        sz = 2 * (number % (nz // 2))
        row = tops[sx, pl.ds(number % (ny * (nz // 2)), 1), :]
        dx = (mx - sx).astype(jnp.float32)
        dy = (my - sy).astype(jnp.float32)
        dz = (mz - sz).astype(jnp.float32) - jnp.where(half, 0.0, 1.0)
        first, second, third = base[0] + dx, base[1] + dy, base[2] + dz
        squared = first * first + second * second + third * third
        reach = jnp.maximum(jnp.maximum(jnp.abs(dx), jnp.abs(dy)), jnp.abs(dz))
        weight = jnp.where(reach >= 2.0, row * INV_FOUR_PI, 0.0)
        kernel = jnp.where(reach >= 2.0, lax.rsqrt(squared), 0.0)
        return value + kernel * weight

    checks = lax.fori_loop(0, nx * ny * (nz // 2), far_turn, jnp.zeros((Q, 128), jnp.float32))
    top_local = jnp.sum(dot(checks.T, fit[...]), axis=0, keepdims=True)

    fitted = jnp.concatenate(
        [dot(total[:, 128 * pair : 128 * pair + 128], pair_fit[...]) for pair in range(4)], axis=1
    )
    line = fitted[72:80] + dot(jnp.broadcast_to(top_local, (8, Q)), down[...])
    order = [2 * c + z for z in range(2) for c in range(4)]
    boxes = jnp.concatenate([line[0:1, Q * c : Q * c + Q] for c in order], axis=0)
    boxes = fitted[64:72] + dot(boxes, down[...])
    for c in range(4):
        for z in range(4):
            column = Q * (2 * c + z % 2)
            stage[16 * c + 4 * z : 16 * c + 4 * z + 4, 0:Q] = boxes[
                4 * (z // 2) : 4 * (z // 2) + 4, column : column + Q
            ]
    lines = fitted[0:64] + dot(stage[0:64, 0:Q], down[...])
    for h in range(4):
        local[h] = lines[:, 128 * h : 128 * h + 128]

    even = lanes() % 2 == 0
    for b in range(4):
        for h in range(4):
            for cy in range(2):
                for gy in range(2):
                    start_row = 16 * (2 * (b % 2) + cy) + 2 * (b // 2) + gy
                    piece = local[h, pl.ds(start_row, 4, stride=4), :]
                    target = 64 * (h // 2) + 8 * (2 * (cy + 2 * gy) + h % 2)
                    stage[pl.ds(target, 4, stride=2), :] = piece
                    stage[pl.ds(target + 1, 4, stride=2), :] = piece
        turned = stage[...].T
        rows[0:Q] = jnp.where(even, turned[0:Q], turned[Q : 2 * Q])
        position = own[b]
        tx, ty, tz = -2.0 * position[0:32], -2.0 * position[32:64], -2.0 * position[64:96]
        squared = 0.25 * (tx * tx + ty * ty + tz * tz) + OUTER * OUTER

        def point_turn(k, value):
            distance = squared + (
                tx * spread[0, pl.ds(k, 1), :]
                + ty * spread[1, pl.ds(k, 1), :]
                + tz * spread[2, pl.ds(k, 1), :]
            )
            return value + lax.rsqrt(distance) * rows[pl.ds(k, 1), :]

        value = lax.fori_loop(0, Q, point_turn, near_sum[b], unroll=16)
        spread_out(value, potential, b)


def per_device(particles, counts):
    spread, fit_twice, up, base, fit, pair_fit, down, high, low = constant_tables()
    sizes = tuple(lax.axis_size(axis) for axis in AXES)
    nx, ny, nz = sizes
    copies = 20 + sum(sizes) - 3
    vmem = pl.BlockSpec(memory_space=pltpu.VMEM)
    remote = pl.BlockSpec(memory_space=pl.ANY)
    single = jnp.float32

    def array(*shape):
        return pltpu.VMEM(shape, single)

    outputs = pl.pallas_call(
        functools.partial(fused_kernel, sizes),
        out_shape=(jax.ShapeDtypeStruct((8, 8, 256), single),) * 2,
        in_specs=[vmem] * 2 + [remote] * 9,
        out_specs=(vmem, vmem),
        scratch_shapes=[
            array(*spread.shape),
            array(*fit_twice.shape),
            array(*up.shape),
            array(*base.shape),
            array(*fit.shape),
            array(*pair_fit.shape),
            array(*down.shape),
            array(10, 160, 128),
            array(3, 10, 160, 128),
            array(3, 10, 160, 128),
            array(4, 128, 128),
            array(4, 96, 128),
            array(160, 128),
            array(160, 128),
            array(160, 128),
            array(160, 128),
            array(160, 128),
            array(6, 12, 12, 128),
            array(4, 8, 8, 128),
            array(3, 6, 6, 128),
            array(nz, 8, 128),
            array(ny, -(-nz // 16) * 8, 128),
            array(nx, -(-ny * nz // 16) * 8, 128),
            array(128, 128),
            array(64, 512),
            array(2, 64, 128),
            array(2, 64, 128),
            array(2, 144, 128),
            array(2, 144, 128),
            array(8, 24, 128),
            array(6, 16, 128),
            pltpu.VMEM((2, 8, 8, 16, 384), jnp.bfloat16),
            pltpu.VMEM((2, 6, 6, 16, 384), jnp.bfloat16),
            array(80, 512),
            array(4, 32, 128),
            array(4, 64, 128),
            pltpu.VMEM(high.shape, jnp.bfloat16),
            pltpu.VMEM(low.shape, jnp.bfloat16),
            pltpu.SemaphoreType.DMA((copies,)),
            pltpu.SemaphoreType.DMA((copies,)),
            pltpu.SemaphoreType.DMA((9,)),
        ],
        compiler_params=pltpu.CompilerParams(
            collective_id=0, has_side_effects=True, vmem_limit_bytes=56 << 20
        ),
        cost_estimate=pl.CostEstimate(flops=8 << 30, bytes_accessed=12 << 20, transcendentals=0),
    )(particles, counts, spread, fit_twice, up, base, fit, pair_fit, down, high, low)
    return tuple(INV_FOUR_PI * output for output in outputs)


def solution(mesh):
    placed = (P("gx", "gy", "gz", None), P("gx", "gy", "gz"))
    return jax.shard_map(
        per_device,
        mesh=mesh,
        in_specs=placed,
        out_specs=(P("gx", "gy", "gz"), P("gx", "gy", "gz")),
        check_vma=False,
    )
```

```python
import functools
import math

import jax
import jax.numpy as jnp
import ml_dtypes
import numpy as np
from jax import lax
from jax.experimental import pallas as pl
from jax.experimental.pallas import tpu as pltpu
from jax.sharding import PartitionSpec as P

Q = 64
INV_FOUR_PI = 0.07957747154594767
INNER = 0.9
OUTER = 1.5
PARENT_CHECK = 3.0
SOFTEN_SQUARED = 0.0625
REGULAR = 0.01
HIGHEST = lax.Precision.HIGHEST
MESH = pl.DeviceIdType.MESH
AXES = ("gx", "gy", "gz")


def sphere(number):
    order = np.arange(number, dtype=np.float64)
    height = 1.0 - (2.0 * order + 1.0) / number
    radial = np.sqrt(1.0 - height * height)
    turning = order * (math.pi * (3.0 - math.sqrt(5.0)))
    return np.stack([radial * np.cos(turning), radial * np.sin(turning), height])


def green(vectors):
    return INV_FOUR_PI / np.sqrt(np.sum(vectors * vectors, axis=0))


def constant_tables():
    points = sphere(Q)
    kernel = green(OUTER * points[:, :, None] - INNER * points[:, None, :])
    normal = kernel.T @ kernel
    normal = normal + REGULAR * np.trace(normal) / Q * np.eye(Q)
    lower = np.linalg.cholesky(normal)
    fit = np.linalg.solve(lower, kernel.T) / np.diag(lower)[:, None]
    up = np.zeros((8 * Q, Q))
    down = np.zeros((Q, 8 * Q))
    for child in range(8):
        offset = np.array([child // 4, child // 2 % 2, child % 2]) - 0.5
        vectors = PARENT_CHECK * points[:, :, None] - INNER * points[:, None, :]
        upper = green(vectors - offset[:, None, None])
        up[child * Q : (child + 1) * Q] = (2.0 * fit @ upper).T
        vectors = INNER * points[:, :, None] - PARENT_CHECK * points[:, None, :]
        lower = green(vectors + offset[:, None, None])
        down[:, child * Q : (child + 1) * Q] = lower.T @ fit
    base = INNER * (points[:, :, None] - points[:, None, :])
    table = np.zeros((7, 7, 6, Q, 2, Q), np.float32)
    for ox in range(-3, 4):
        for oy in range(-3, 4):
            for sz in range(6):
                for cz in range(2):
                    offset = np.array([ox, oy, sz - 2 - cz], np.float64)
                    if np.max(np.abs(offset)) >= 2:
                        values = green(base - offset[:, None, None])
                        table[ox + 3, oy + 3, sz, :, cz, :] = values.T
    table = table.reshape(7, 7, 6 * Q, 2 * Q)
    high = table.astype(ml_dtypes.bfloat16)
    low = (table - high.astype(np.float32)).astype(ml_dtypes.bfloat16)
    spread = np.repeat((OUTER * points)[:, :, None], 128, axis=2)
    single = np.float32
    return (
        spread.astype(single),
        np.tile(fit.T, (1, 2)).astype(single),
        np.tile(up, (1, 2)).astype(single),
        np.tile(base, (1, 1, 2)).astype(single),
        fit.astype(single),
        np.kron(np.eye(2), fit).astype(single),
        down.astype(single),
        high,
        low,
    )


def dot(left, right):
    return jnp.dot(left, right, precision=HIGHEST, preferred_element_type=jnp.float32)


def lanes(shape=(1, 128)):
    return lax.broadcasted_iota(jnp.int32, shape, 1)


def fused_kernel(
    sizes,
    part,
    counts,
    spread_far,
    fit_twice_far,
    up_far,
    base_far,
    fit_far,
    pair_fit_far,
    down_far,
    high_far,
    low_far,
    potential,
    near_out,
    spread,
    fit_twice,
    up,
    base,
    fit,
    pair_fit,
    down,
    cells,
    planes,
    edges,
    own,
    own_twice,
    rows,
    slab0,
    slab1,
    slab2,
    slab3,
    leaf,
    mid,
    coarse,
    tops_z,
    tops_y,
    tops,
    stage,
    lift_rows,
    pz_out,
    pz_in,
    my_out,
    my_in,
    gather,
    gather_mid,
    wide,
    narrow,
    total,
    near_sum,
    local,
    high,
    low,
    send_sem,
    recv_sem,
    table_sem,
):
    nx, ny, nz = sizes
    place = {axis: lax.axis_index(axis) for axis in AXES}
    count = dict(zip(AXES, sizes))
    mx, my, mz = (place[axis] for axis in AXES)
    half = lanes() < Q

    pairs = (
        (spread_far, spread),
        (fit_twice_far, fit_twice),
        (up_far, up),
        (base_far, base),
        (fit_far, fit),
        (pair_fit_far, pair_fit),
        (down_far, down),
        (high_far, high),
        (low_far, low),
    )
    tables = [
        pltpu.make_async_copy(far, here, table_sem.at[number])
        for number, (far, here) in enumerate(pairs)
    ]
    for table in tables:
        table.start()

    def clear(ref):
        def turn(number, carry):
            ref[number] = jnp.zeros(ref.shape[1:], jnp.float32)
            return carry

        lax.fori_loop(0, ref.shape[0], turn, 0)

    for ref in (cells, leaf, mid, coarse, my_out, tops_y, tops):
        clear(ref)

    barrier = pltpu.get_barrier_semaphore()
    mates = [
        (axis, lax.rem(place[axis] + step, count[axis]))
        for axis in AXES
        for step in range(1, count[axis])
    ]
    for axis, mate in mates:
        pl.semaphore_signal(barrier, inc=1, device_id={axis: mate}, device_id_type=MESH)

    class Shift:
        def __init__(self, axis, step, index, source, target):
            m, n = place[axis], count[axis]
            first, last = m > 0, m < n - 1
            self.sends, self.receives = (last, first) if step == 1 else (first, last)
            self.copy = pltpu.make_async_remote_copy(
                src_ref=source,
                dst_ref=target,
                send_sem=send_sem.at[index],
                recv_sem=recv_sem.at[index],
                device_id={axis: lax.rem(m + step + n, n)},
                device_id_type=MESH,
            )

        def start(self):
            pl.when(self.sends)(lambda: self.copy.start())

        def wait(self):
            pl.when(self.sends)(lambda: self.copy.wait_send())
            pl.when(self.receives)(lambda: self.copy.wait_recv())

    class Spread:
        def __init__(self, axis, step, index, block):
            m, n = place[axis], count[axis]
            self.copy = pltpu.make_async_remote_copy(
                src_ref=block,
                dst_ref=block,
                send_sem=send_sem.at[index],
                recv_sem=recv_sem.at[index],
                device_id={axis: lax.rem(m + step, n)},
                device_id_type=MESH,
            )

        def start(self):
            self.copy.start()

        def wait(self):
            self.copy.wait_send()
            self.copy.wait_recv()

    def start(copies):
        for copy in copies:
            copy.start()

    def wait(copies):
        for copy in copies:
            copy.wait()

    slot = lanes((8, 128)) - 96
    square = lax.broadcasted_iota(jnp.int32, (8, 8), 0) == lax.broadcasted_iota(jnp.int32, (8, 8), 1)

    def mask_turn(x, carry):
        present = counts[x].astype(jnp.float32)
        for y in range(8):
            line = jnp.where(square, jnp.broadcast_to(present[y : y + 1], (8, 8)), 0.0)
            number = jnp.sum(line, axis=1, keepdims=True)
            values = jnp.where(slot.astype(jnp.float32) < number, part[x, y], 0.0)
            cells[x + 1, 16 * (y + 1) + 1 : 16 * (y + 1) + 9, :] = values
        return carry

    lax.fori_loop(0, 8, mask_turn, 0)
    for x in range(8):
        for side, z in ((0, 8), (1, 1)):
            pz_out[side, 8 * x : 8 * x + 8, :] = cells[x + 1, pl.ds(16 + z, 8, stride=16), :]

    def upward(b):
        pieces = [
            cells[2 * b + 1 + i, 16 * (y + 1) + 1 : 16 * (y + 1) + 9, :]
            for i in range(2)
            for y in range(8)
        ]
        turned = jnp.concatenate(pieces, axis=0).T
        own[b] = turned
        own_twice[b] = -2.0 * turned[0:96]
        tx, ty, tz = turned[0:32], turned[32:64], turned[64:96]
        rows[0:96] = -2.0 * turned[0:96]
        rows[96:128] = turned[96:128] * INV_FOUR_PI
        rows[128:160] = (tx * tx + ty * ty) + (tz * tz + OUTER * OUTER)

        def slot_turn(p, value):
            distance = rows[pl.ds(128 + p, 1), :] + (
                spread[0] * rows[pl.ds(p, 1), :]
                + spread[1] * rows[pl.ds(32 + p, 1), :]
                + spread[2] * rows[pl.ds(64 + p, 1), :]
            )
            return value + lax.rsqrt(distance) * rows[pl.ds(96 + p, 1), :]

        checks = lax.fori_loop(0, 32, slot_turn, jnp.zeros((Q, 128), jnp.float32), unroll=32)
        stage[...] = dot(checks.T, fit_twice[...])
        for i in range(2):
            for pair in range(4):
                even = stage[pl.ds(64 * i + 2 * pair, 8, stride=8), :]
                odd = stage[pl.ds(64 * i + 2 * pair + 1, 8, stride=8), :]
                leaf[pair + 1, 2 * b + i + 2, 2:10, :] = jnp.where(half, even, odd)

    tables[0].wait()
    tables[1].wait()
    for b in range(4):
        upward(b)
    tables[2].wait()

    for c in range(4):
        for z in range(4):
            for x in range(4):
                piece = leaf[z + 1, 2 * x + c // 2 + 2, pl.ds(c % 2 + 2, 4, stride=2), :]
                lift_rows[16 * z + 4 * x : 16 * z + 4 * x + 4, 128 * c : 128 * c + 128] = piece
    stage[0:64] = dot(lift_rows[...], up[...])
    for pair in range(2):
        for x in range(4):
            even = stage[32 * pair + 4 * x : 32 * pair + 4 * x + 4, :]
            odd = stage[32 * pair + 16 + 4 * x : 32 * pair + 16 + 4 * x + 4, :]
            mid[pair + 1, x + 2, 2:6, :] = jnp.where(half, even, odd)
    for c in range(4):
        for z in range(2):
            for x in range(2):
                piece = mid[z + 1, 2 * x + c // 2 + 2, pl.ds(c % 2 + 2, 2, stride=2), :]
                lift_rows[4 * z + 2 * x : 4 * z + 2 * x + 2, 128 * c : 128 * c + 128] = piece
    stage[0:8] = dot(lift_rows[0:8], up[...])
    for x in range(2):
        even, odd = stage[2 * x : 2 * x + 2, :], stage[4 + 2 * x : 4 + 2 * x + 2, :]
        coarse[1, x + 2, 2:4, :] = jnp.where(half, even, odd)
    line = jnp.concatenate(
        [coarse[1, c // 2 + 2, c % 2 + 2 : c % 2 + 3, :] for c in range(4)], axis=1
    )
    tops_z[mz] = dot(jnp.broadcast_to(line, (8, 8 * Q)), up[...])

    pl.semaphore_wait(barrier, len(mates))
    multi = [
        Shift("gz", 1, 6, leaf.at[4, pl.ds(2, 8)], leaf.at[0, pl.ds(2, 8)]),
        Shift("gz", -1, 7, leaf.at[1, pl.ds(2, 8)], leaf.at[5, pl.ds(2, 8)]),
        Shift("gz", 1, 8, mid.at[2, pl.ds(2, 4)], mid.at[0, pl.ds(2, 4)]),
        Shift("gz", -1, 9, mid.at[1, pl.ds(2, 4)], mid.at[3, pl.ds(2, 4)]),
        Shift("gz", 1, 10, coarse.at[1, pl.ds(2, 2)], coarse.at[0, pl.ds(2, 2)]),
        Shift("gz", -1, 11, coarse.at[1, pl.ds(2, 2)], coarse.at[2, pl.ds(2, 2)]),
    ]
    index = 20
    for step in range(1, nz):
        multi.append(Spread("gz", step, index, tops_z.at[mz]))
        index += 1
    start(multi)
    shifts = [Shift("gz", 1 - 2 * s, s, pz_out.at[s], pz_in.at[s]) for s in range(2)]
    start(shifts)
    wait(multi)
    for pair in range(nz // 2):
        even, odd = tops_z[2 * pair, 0:1, :], tops_z[2 * pair + 1, 0:1, :]
        tops_y[my, pair : pair + 1, :] = jnp.where(half, even, odd)
    packed = []
    for ref, tiles, width in ((leaf, 6, 8), (mid, 4, 4), (coarse, 3, 2)):
        for tile in range(tiles):
            for x in range(width):
                packed.append((ref, tile, x + 2, width))
    for number, (ref, tile, x, width) in enumerate(packed):
        my_out[0, 2 * number : 2 * number + 2, :] = ref[tile, x, width : width + 2, :]
        my_out[1, 2 * number : 2 * number + 2, :] = ref[tile, x, 2:4, :]
    multi = [Shift("gy", 1 - 2 * s, 12 + s, my_out.at[s], my_in.at[s]) for s in range(2)]
    for step in range(1, ny):
        multi.append(Spread("gy", step, index, tops_y.at[my]))
        index += 1
    start(multi)

    wait(shifts)

    @pl.when(mz > 0)
    def _():
        for x in range(8):
            cells[x + 1, pl.ds(16, 8, stride=16), :] = pz_in[0, 8 * x : 8 * x + 8, :]

    @pl.when(mz < nz - 1)
    def _():
        for x in range(8):
            cells[x + 1, pl.ds(16 + 9, 8, stride=16), :] = pz_in[1, 8 * x : 8 * x + 8, :]

    inner = pl.ds(1, 8)
    shifts = [
        Shift("gy", 1, 2, cells.at[inner, pl.ds(128, 16)], cells.at[inner, pl.ds(0, 16)]),
        Shift("gy", -1, 3, cells.at[inner, pl.ds(16, 16)], cells.at[inner, pl.ds(144, 16)]),
    ]
    start(shifts)
    def put(target, pieces):
        turned = jnp.concatenate(pieces, axis=0).T
        sx, sy, sz = turned[0:32], turned[32:64], turned[64:96]
        target[0:128] = turned
        target[128:160] = (sx * sx + sy * sy) + sz * sz

    def column(x, y, oz):
        return cells[x, 16 * y + oz : 16 * y + oz + 8, :]

    def pair_turn(first, second, entry):
        for oz in range(3):
            put(planes.at[oz, entry], [column(x, y + 1, oz) for x in (first, second) for y in range(8)])

    def edge_turn(first, second, entry):
        for oz in range(3):
            pieces = []
            for x in (first, second):
                pieces += [column(x, 0, oz)] * 4 + [column(x, 9, oz)] * 4
            put(edges.at[oz, entry], pieces)

    def between(ref, low_entry, high_entry, entry):
        for oz in range(3):
            both = jnp.where(half, ref[oz, high_entry], ref[oz, low_entry])
            ref[oz, entry] = pltpu.roll(both, Q, 1)

    def pair_loop(k, carry):
        pair_turn(2 * k + 1, 2 * k + 2, 2 * k + 1)
        return carry

    def edge_loop(k, carry):
        edge_turn(2 * k + 1, 2 * k + 2, 2 * k + 1)
        return carry

    def between_loop(ref):
        def turn(k, carry):
            between(ref, 2 * k + 1, 2 * k + 3, 2 * k + 2)
            return carry

        lax.fori_loop(0, 3, turn, 0)

    group = lanes((8, 128)) // 32
    inside = lanes() % Q

    def spread_out(values, target, b):
        stage[...] = jnp.concatenate([values] * 4, axis=0).T
        for i in range(2):
            for block in range(2):
                result = None
                for z in range(4):
                    line = stage[pl.ds(64 * i + 4 * block + z, 8, stride=8), :]
                    result = line if z == 0 else jnp.where(group == z, line, result)
                target[2 * b + i, :, 128 * block : 128 * block + 128] = result

    def fill(target, entry, oz, oy):
        if oy < 0:
            target[...] = jnp.where(inside < 8, edges[oz, entry], pltpu.roll(planes[oz, entry], 8, 1))
        else:
            target[...] = jnp.where(
                inside >= 56, edges[oz, entry], pltpu.roll(planes[oz, entry], 120, 1)
            )

    def add(source, moves, oz, oy):
        sides = []
        dz = 2.0 * (oz - 1).astype(jnp.float32)
        for b, ox in moves:
            x = own_twice[b, 0:32] + 2.0 * ox
            y = own_twice[b, 32:64] + 2.0 * oy
            z = own_twice[b, 64:96] + dz
            sides.append((x, y, z, 0.25 * (x * x + y * y + z * z) + SOFTEN_SQUARED))

        def source_turn(p, values):
            sx, sy, sz = (source[pl.ds(32 * c + p, 1), :] for c in range(3))
            strength, length = source[pl.ds(96 + p, 1), :], source[pl.ds(128 + p, 1), :]
            result = []
            for (x, y, z, squared), value in zip(sides, values):
                distance = (squared + length) + (x * sx + y * sy + z * sz)
                result.append(value + lax.rsqrt(distance) * strength)
            return tuple(result)

        zero = jnp.zeros((32, 128), jnp.float32)
        values = lax.fori_loop(0, 32, source_turn, (zero,) * len(moves), unroll=32)
        for (b, ox), value in zip(moves, values):
            near_sum[b] += value

    def single_moves(k):
        return 2 * k + 1, [(k, 0.0)]

    def double_moves(k):
        return 2 * k + 2, [(k + 1, -1.0), (k, 1.0)]

    near_sum[...] = jnp.zeros_like(near_sum)
    lax.fori_loop(0, 4, pair_loop, 0)
    between_loop(planes)

    def straight_turn(number, carry):
        for oz in range(3):
            for entry, moves in (single_moves(number), double_moves(number)):
                add(planes.at[oz, entry], moves, jnp.int32(oz), 0)
        return carry

    lax.fori_loop(0, 1, straight_turn, 0)
    wait(multi)
    for y in range(ny):
        tops[mx, y * (nz // 2) : (y + 1) * (nz // 2), :] = tops_y[y, 0 : nz // 2, :]

    @pl.when(my > 0)
    def _():
        for number, (ref, tile, x, width) in enumerate(packed):
            ref[tile, x, 0:2, :] = my_in[0, 2 * number : 2 * number + 2, :]

    @pl.when(my < ny - 1)
    def _():
        for number, (ref, tile, x, width) in enumerate(packed):
            ref[tile, x, width + 2 : width + 4, :] = my_in[1, 2 * number : 2 * number + 2, :]

    multi = []
    for number, (ref, tiles, width) in enumerate(((leaf, 6, 8), (mid, 4, 4), (coarse, 3, 2))):
        every = pl.ds(0, tiles)
        left, right = ref.at[every, pl.ds(0, 2)], ref.at[every, pl.ds(width + 2, 2)]
        multi.append(Shift("gx", 1, 14 + 2 * number, ref.at[every, pl.ds(width, 2)], left))
        multi.append(Shift("gx", -1, 15 + 2 * number, ref.at[every, pl.ds(2, 2)], right))
    for step in range(1, nx):
        multi.append(Spread("gx", step, index, tops.at[mx]))
        index += 1
    start(multi)
    lax.fori_loop(1, 3, straight_turn, 0)
    for oz in range(3):
        add(planes.at[oz, 7], [(3, 0.0)], jnp.int32(oz), 0)

    wait(shifts)
    shifts = [
        Shift("gx", 1, 4, cells.at[8], cells.at[0]),
        Shift("gx", -1, 5, cells.at[1], cells.at[9]),
    ]
    start(shifts)
    lax.fori_loop(0, 4, edge_loop, 0)
    between_loop(edges)

    def shifted(parts, oz):
        slabs = iter((slab0, slab1, slab2, slab3))
        jobs = [(next(slabs), entry, moves, oy) for entry, moves in parts for oy in (-1, 1)]
        for slab, entry, moves, oy in jobs:
            fill(slab, entry, oz, oy)
        for slab, entry, moves, oy in jobs:
            add(slab, moves, oz, oy)

    def shifted_turn(number, carry):
        k = number // 3
        shifted([single_moves(k), double_moves(k)], number % 3)
        return carry

    lax.fori_loop(0, 6, shifted_turn, 0)
    wait(multi)
    for table in tables[3:]:
        table.wait()

    def split(values):
        first = values.astype(jnp.bfloat16)
        return first, (values - first.astype(jnp.float32)).astype(jnp.bfloat16)

    def wide_turn(ux, carry):
        for uy in range(8):
            for tile in range(6):
                for gx in range(2):
                    piece = leaf[tile, ux + 4 * gx, pl.ds(uy, 2, stride=4), :]
                    gather[uy, 4 * tile + 2 * gx : 4 * tile + 2 * gx + 2, :] = piece
        for uy in range(8):
            for t in range(3):
                first, second = split(gather[uy, 4 * t : 4 * t + 16, :])
                wide[0, ux, uy, :, 128 * t : 128 * t + 128] = first
                wide[1, ux, uy, :, 128 * t : 128 * t + 128] = second
        return carry

    lax.fori_loop(0, 8, wide_turn, 0)

    def narrow_turn(sx, carry):
        for sy in range(6):
            for tile in range(4):
                for gx in range(2):
                    piece = mid[tile, sx + 2 * gx, pl.ds(sy, 2, stride=2), :]
                    gather_mid[sy, 4 * tile + 2 * gx : 4 * tile + 2 * gx + 2, :] = piece
        for sy in range(6):
            for t in range(3):
                last = jnp.broadcast_to(coarse[t, sx, sy : sy + 1, :], (8, 128))
                both = jnp.concatenate([gather_mid[sy, 4 * t : 4 * t + 8, :], last], axis=0)
                first, second = split(both)
                narrow[0, sx, sy, :, 128 * t : 128 * t + 128] = first
                narrow[1, sx, sy, :, 128 * t : 128 * t + 128] = second
        return carry

    lax.fori_loop(0, 6, narrow_turn, 0)
    total[...] = jnp.zeros_like(total)

    def list_part(number):
        sx = number // 3
        lefts = []
        for k in range(2):
            sy = 2 * (number % 3) + k
            columns = []
            for h in range(2):
                columns += [wide[h, sx + 2 * (c // 2), sy + 2 * (c % 2)] for c in range(4)]
                columns.append(narrow[h, sx, sy])
            lefts.append(jnp.concatenate(columns, axis=0))
        left = jnp.concatenate(lefts, axis=1)
        for cx in range(2):

            def right(table):
                lines = []
                for k in range(2):
                    sy = 2 * (number % 3) + k
                    pieces = [table[sx + 1 - cx, sy + 1 - cy] for cy in range(2)]
                    lines.append(jnp.concatenate(pieces, axis=1))
                return jnp.concatenate(lines, axis=0)

            first = jnp.dot(left, right(high), preferred_element_type=jnp.float32)
            second = jnp.dot(left[:80], right(low), preferred_element_type=jnp.float32)
            total[:, 256 * cx : 256 * cx + 256] += first[:80] + first[80:] + second

    def mixed_turn(number, carry):
        list_part(2 * number)
        list_part(2 * number + 1)
        return shifted_turn(number + 6, carry)

    lax.fori_loop(0, 3, mixed_turn, 0)

    def last_turn(oz, carry):
        list_part(2 * oz + 6)
        list_part(2 * oz + 7)
        shifted([single_moves(3)], oz)
        return carry

    lax.fori_loop(0, 3, last_turn, 0)

    wait(shifts)
    for turn, ref in ((pair_turn, planes), (edge_turn, edges)):
        turn(9, 0, 9)
        between(ref, 9, 1, 0)
        between(ref, 7, 9, 8)

    def outer_turn(oz, carry):
        for k, part in enumerate(((0, [(0, -1.0)]), (8, [(3, 1.0)]))):
            list_part(2 * oz + 12 + k)
            entry, moves = part
            add(planes.at[oz, entry], moves, oz, 0)
            shifted([part], oz)
        return carry

    lax.fori_loop(0, 3, outer_turn, 0)
    for b in range(4):
        spread_out(near_sum[b], near_out, b)

    def far_turn(number, value):
        sx = number // (ny * (nz // 2))
        sy = number // (nz // 2) % ny
        sz = 2 * (number % (nz // 2))
        row = tops[sx, pl.ds(number % (ny * (nz // 2)), 1), :]
        dx = (mx - sx).astype(jnp.float32)
        dy = (my - sy).astype(jnp.float32)
        dz = (mz - sz).astype(jnp.float32) - jnp.where(half, 0.0, 1.0)
        first, second, third = base[0] + dx, base[1] + dy, base[2] + dz
        squared = first * first + second * second + third * third
        reach = jnp.maximum(jnp.maximum(jnp.abs(dx), jnp.abs(dy)), jnp.abs(dz))
        weight = jnp.where(reach >= 2.0, row * INV_FOUR_PI, 0.0)
        kernel = jnp.where(reach >= 2.0, lax.rsqrt(squared), 0.0)
        return value + kernel * weight

    checks = lax.fori_loop(0, nx * ny * (nz // 2), far_turn, jnp.zeros((Q, 128), jnp.float32))
    top_local = jnp.sum(dot(checks.T, fit[...]), axis=0, keepdims=True)

    fitted = jnp.concatenate(
        [dot(total[:, 128 * pair : 128 * pair + 128], pair_fit[...]) for pair in range(4)], axis=1
    )
    line = fitted[72:80] + dot(jnp.broadcast_to(top_local, (8, Q)), down[...])
    order = [2 * c + z for z in range(2) for c in range(4)]
    boxes = jnp.concatenate([line[0:1, Q * c : Q * c + Q] for c in order], axis=0)
    boxes = fitted[64:72] + dot(boxes, down[...])
    for c in range(4):
        for z in range(4):
            column = Q * (2 * c + z % 2)
            stage[16 * c + 4 * z : 16 * c + 4 * z + 4, 0:Q] = boxes[
                4 * (z // 2) : 4 * (z // 2) + 4, column : column + Q
            ]
    lines = fitted[0:64] + dot(stage[0:64, 0:Q], down[...])
    for h in range(4):
        local[h] = lines[:, 128 * h : 128 * h + 128]

    even = lanes() % 2 == 0
    slabs = (slab0, slab1, slab2, slab3)
    for b in range(4):
        for h in range(4):
            for cy in range(2):
                for gy in range(2):
                    start_row = 16 * (2 * (b % 2) + cy) + 2 * (b // 2) + gy
                    piece = local[h, pl.ds(start_row, 4, stride=4), :]
                    target = 64 * (h // 2) + 8 * (2 * (cy + 2 * gy) + h % 2)
                    stage[pl.ds(target, 4, stride=2), :] = piece
                    stage[pl.ds(target + 1, 4, stride=2), :] = piece
        turned = stage[...].T
        slabs[b][0:Q] = jnp.where(even, turned[0:Q], turned[Q : 2 * Q])

    for pair in range(2):
        sides = []
        for b in (2 * pair, 2 * pair + 1):
            x, y, z = own_twice[b, 0:32], own_twice[b, 32:64], own_twice[b, 64:96]
            sides.append((x, y, z, 0.25 * (x * x + y * y + z * z) + OUTER * OUTER, slabs[b]))

        def point_turn(k, values):
            px, py, pz = (spread[c, pl.ds(k, 1), :] for c in range(3))
            result = []
            for (x, y, z, squared, density), value in zip(sides, values):
                distance = squared + (x * px + y * py + z * pz)
                result.append(value + lax.rsqrt(distance) * density[pl.ds(k, 1), :])
            return tuple(result)

        first = (near_sum[2 * pair], near_sum[2 * pair + 1])
        values = lax.fori_loop(0, Q, point_turn, first, unroll=32)
        for b, value in zip((2 * pair, 2 * pair + 1), values):
            spread_out(value, potential, b)


def per_device(particles, counts):
    spread, fit_twice, up, base, fit, pair_fit, down, high, low = constant_tables()
    sizes = tuple(lax.axis_size(axis) for axis in AXES)
    nx, ny, nz = sizes
    copies = 20 + sum(sizes) - 3
    vmem = pl.BlockSpec(memory_space=pltpu.VMEM)
    remote = pl.BlockSpec(memory_space=pl.ANY)
    single = jnp.float32

    def array(*shape):
        return pltpu.VMEM(shape, single)

    outputs = pl.pallas_call(
        functools.partial(fused_kernel, sizes),
        out_shape=(jax.ShapeDtypeStruct((8, 8, 256), single),) * 2,
        in_specs=[vmem] * 2 + [remote] * 9,
        out_specs=(vmem, vmem),
        scratch_shapes=[
            array(*spread.shape),
            array(*fit_twice.shape),
            array(*up.shape),
            array(*base.shape),
            array(*fit.shape),
            array(*pair_fit.shape),
            array(*down.shape),
            array(10, 160, 128),
            array(3, 10, 160, 128),
            array(3, 10, 160, 128),
            array(4, 128, 128),
            array(4, 96, 128),
            array(160, 128),
            array(160, 128),
            array(160, 128),
            array(160, 128),
            array(160, 128),
            array(6, 12, 12, 128),
            array(4, 8, 8, 128),
            array(3, 6, 6, 128),
            array(nz, 8, 128),
            array(ny, -(-nz // 16) * 8, 128),
            array(nx, -(-ny * nz // 16) * 8, 128),
            array(128, 128),
            array(64, 512),
            array(2, 64, 128),
            array(2, 64, 128),
            array(2, 144, 128),
            array(2, 144, 128),
            array(8, 24, 128),
            array(6, 16, 128),
            pltpu.VMEM((2, 8, 8, 16, 384), jnp.bfloat16),
            pltpu.VMEM((2, 6, 6, 16, 384), jnp.bfloat16),
            array(80, 512),
            array(4, 32, 128),
            array(4, 64, 128),
            pltpu.VMEM(high.shape, jnp.bfloat16),
            pltpu.VMEM(low.shape, jnp.bfloat16),
            pltpu.SemaphoreType.DMA((copies,)),
            pltpu.SemaphoreType.DMA((copies,)),
            pltpu.SemaphoreType.DMA((9,)),
        ],
        compiler_params=pltpu.CompilerParams(
            collective_id=0, has_side_effects=True, vmem_limit_bytes=56 << 20
        ),
        cost_estimate=pl.CostEstimate(flops=8 << 30, bytes_accessed=12 << 20, transcendentals=0),
    )(particles, counts, spread, fit_twice, up, base, fit, pair_fit, down, high, low)
    return tuple(INV_FOUR_PI * output for output in outputs)


def solution(mesh):
    placed = (P("gx", "gy", "gz", None), P("gx", "gy", "gz"))
    return jax.shard_map(
        per_device,
        mesh=mesh,
        in_specs=placed,
        out_specs=(P("gx", "gy", "gz"), P("gx", "gy", "gz")),
        check_vma=False,
    )
```

```python
import functools
import math

import jax
import jax.numpy as jnp
import ml_dtypes
import numpy as np
from jax import lax
from jax.experimental import pallas as pl
from jax.experimental.pallas import tpu as pltpu
from jax.sharding import PartitionSpec as P

Q = 64
INV_FOUR_PI = 0.07957747154594767
INNER = 0.9
OUTER = 1.5
PARENT_CHECK = 3.0
SOFTEN_SQUARED = 0.0625
REGULAR = 0.01
HIGHEST = lax.Precision.HIGHEST
MESH = pl.DeviceIdType.MESH
AXES = ("gx", "gy", "gz")


def sphere(number):
    order = np.arange(number, dtype=np.float64)
    height = 1.0 - (2.0 * order + 1.0) / number
    radial = np.sqrt(1.0 - height * height)
    turning = order * (math.pi * (3.0 - math.sqrt(5.0)))
    return np.stack([radial * np.cos(turning), radial * np.sin(turning), height])


def green(vectors):
    return INV_FOUR_PI / np.sqrt(np.sum(vectors * vectors, axis=0))


def constant_tables():
    points = sphere(Q)
    kernel = green(OUTER * points[:, :, None] - INNER * points[:, None, :])
    normal = kernel.T @ kernel
    normal = normal + REGULAR * np.trace(normal) / Q * np.eye(Q)
    lower = np.linalg.cholesky(normal)
    fit = np.linalg.solve(lower, kernel.T) / np.diag(lower)[:, None]
    up = np.zeros((8 * Q, Q))
    down = np.zeros((Q, 8 * Q))
    for child in range(8):
        offset = np.array([child // 4, child // 2 % 2, child % 2]) - 0.5
        vectors = PARENT_CHECK * points[:, :, None] - INNER * points[:, None, :]
        upper = green(vectors - offset[:, None, None])
        up[child * Q : (child + 1) * Q] = (2.0 * fit @ upper).T
        vectors = INNER * points[:, :, None] - PARENT_CHECK * points[:, None, :]
        lower = green(vectors + offset[:, None, None])
        down[:, child * Q : (child + 1) * Q] = lower.T @ fit
    base = INNER * (points[:, :, None] - points[:, None, :])
    table = np.zeros((7, 7, 6, Q, 2, Q), np.float32)
    for ox in range(-3, 4):
        for oy in range(-3, 4):
            for sz in range(6):
                for cz in range(2):
                    offset = np.array([ox, oy, sz - 2 - cz], np.float64)
                    if np.max(np.abs(offset)) >= 2:
                        values = green(base - offset[:, None, None])
                        table[ox + 3, oy + 3, sz, :, cz, :] = values.T
    table = table.reshape(7, 7, 6 * Q, 2 * Q)
    high = table.astype(ml_dtypes.bfloat16)
    low = (table - high.astype(np.float32)).astype(ml_dtypes.bfloat16)
    spread = np.repeat((OUTER * points)[:, :, None], 128, axis=2)
    single = np.float32
    return (
        spread.astype(single),
        np.tile(fit.T, (1, 2)).astype(single),
        np.tile(up, (1, 2)).astype(single),
        np.tile(base, (1, 1, 2)).astype(single),
        fit.astype(single),
        np.kron(np.eye(2), fit).astype(single),
        down.astype(single),
        high,
        low,
    )


def dot(left, right):
    return jnp.dot(left, right, precision=HIGHEST, preferred_element_type=jnp.float32)


def lanes(shape=(1, 128)):
    return lax.broadcasted_iota(jnp.int32, shape, 1)


def fused_kernel(
    sizes,
    part,
    counts,
    spread_far,
    fit_twice_far,
    up_far,
    base_far,
    fit_far,
    pair_fit_far,
    down_far,
    high_far,
    low_far,
    potential,
    near_out,
    spread,
    fit_twice,
    up,
    base,
    fit,
    pair_fit,
    down,
    cells,
    planes,
    edges,
    own,
    own_twice,
    rows,
    slab0,
    slab1,
    slab2,
    slab3,
    leaf,
    mid,
    coarse,
    tops_z,
    tops_y,
    tops,
    stage,
    lift_rows,
    pz_out,
    pz_in,
    my_out,
    my_in,
    gather,
    gather_mid,
    wide,
    narrow,
    total,
    near_sum,
    local,
    high,
    low,
    send_sem,
    recv_sem,
    table_sem,
):
    nx, ny, nz = sizes
    place = {axis: lax.axis_index(axis) for axis in AXES}
    count = dict(zip(AXES, sizes))
    mx, my, mz = (place[axis] for axis in AXES)
    half = lanes() < Q

    pairs = (
        (spread_far, spread),
        (fit_twice_far, fit_twice),
        (up_far, up),
        (base_far, base),
        (fit_far, fit),
        (pair_fit_far, pair_fit),
        (down_far, down),
        (high_far, high),
        (low_far, low),
    )
    tables = [
        pltpu.make_async_copy(far, here, table_sem.at[number])
        for number, (far, here) in enumerate(pairs)
    ]
    for table in tables:
        table.start()

    def clear(ref):
        def turn(number, carry):
            ref[number] = jnp.zeros(ref.shape[1:], jnp.float32)
            return carry

        lax.fori_loop(0, ref.shape[0], turn, 0)

    for ref in (cells, leaf, mid, coarse, my_out, tops_y, tops):
        clear(ref)

    barrier = pltpu.get_barrier_semaphore()
    mates = [
        (axis, lax.rem(place[axis] + step, count[axis]))
        for axis in AXES
        for step in range(1, count[axis])
    ]
    for axis, mate in mates:
        pl.semaphore_signal(barrier, inc=1, device_id={axis: mate}, device_id_type=MESH)

    class Shift:
        def __init__(self, axis, step, index, source, target):
            m, n = place[axis], count[axis]
            first, last = m > 0, m < n - 1
            self.sends, self.receives = (last, first) if step == 1 else (first, last)
            self.copy = pltpu.make_async_remote_copy(
                src_ref=source,
                dst_ref=target,
                send_sem=send_sem.at[index],
                recv_sem=recv_sem.at[index],
                device_id={axis: lax.rem(m + step + n, n)},
                device_id_type=MESH,
            )

        def start(self):
            pl.when(self.sends)(lambda: self.copy.start())

        def wait(self):
            pl.when(self.sends)(lambda: self.copy.wait_send())
            pl.when(self.receives)(lambda: self.copy.wait_recv())

    class Spread:
        def __init__(self, axis, step, index, block):
            m, n = place[axis], count[axis]
            self.copy = pltpu.make_async_remote_copy(
                src_ref=block,
                dst_ref=block,
                send_sem=send_sem.at[index],
                recv_sem=recv_sem.at[index],
                device_id={axis: lax.rem(m + step, n)},
                device_id_type=MESH,
            )

        def start(self):
            self.copy.start()

        def wait(self):
            self.copy.wait_send()
            self.copy.wait_recv()

    def start(copies):
        for copy in copies:
            copy.start()

    def wait(copies):
        for copy in copies:
            copy.wait()

    slot = lanes((8, 128)) - 96
    square = lax.broadcasted_iota(jnp.int32, (8, 8), 0) == lax.broadcasted_iota(jnp.int32, (8, 8), 1)

    def mask_turn(x, carry):
        present = counts[x].astype(jnp.float32)
        for y in range(8):
            line = jnp.where(square, jnp.broadcast_to(present[y : y + 1], (8, 8)), 0.0)
            number = jnp.sum(line, axis=1, keepdims=True)
            values = jnp.where(slot.astype(jnp.float32) < number, part[x, y], 0.0)
            cells[x + 1, 16 * (y + 1) + 1 : 16 * (y + 1) + 9, :] = values
        return carry

    lax.fori_loop(0, 8, mask_turn, 0)
    for x in range(8):
        for side, z in ((0, 8), (1, 1)):
            pz_out[side, 8 * x : 8 * x + 8, :] = cells[x + 1, pl.ds(16 + z, 8, stride=16), :]

    def upward(b):
        pieces = [
            cells[2 * b + 1 + i, 16 * (y + 1) + 1 : 16 * (y + 1) + 9, :]
            for i in range(2)
            for y in range(8)
        ]
        turned = jnp.concatenate(pieces, axis=0).T
        own[b] = turned
        own_twice[b] = -2.0 * turned[0:96]
        tx, ty, tz = turned[0:32], turned[32:64], turned[64:96]
        rows[0:96] = -2.0 * turned[0:96]
        rows[96:128] = turned[96:128] * INV_FOUR_PI
        rows[128:160] = (tx * tx + ty * ty) + (tz * tz + OUTER * OUTER)

        def slot_turn(p, value):
            distance = rows[pl.ds(128 + p, 1), :] + (
                spread[0] * rows[pl.ds(p, 1), :]
                + spread[1] * rows[pl.ds(32 + p, 1), :]
                + spread[2] * rows[pl.ds(64 + p, 1), :]
            )
            return value + lax.rsqrt(distance) * rows[pl.ds(96 + p, 1), :]

        checks = lax.fori_loop(0, 32, slot_turn, jnp.zeros((Q, 128), jnp.float32), unroll=32)
        stage[...] = dot(checks.T, fit_twice[...])
        for i in range(2):
            for pair in range(4):
                even = stage[pl.ds(64 * i + 2 * pair, 8, stride=8), :]
                odd = stage[pl.ds(64 * i + 2 * pair + 1, 8, stride=8), :]
                leaf[pair + 1, 2 * b + i + 2, 2:10, :] = jnp.where(half, even, odd)

    tables[0].wait()
    tables[1].wait()
    for b in range(4):
        upward(b)
    tables[2].wait()

    for c in range(4):
        for z in range(4):
            for x in range(4):
                piece = leaf[z + 1, 2 * x + c // 2 + 2, pl.ds(c % 2 + 2, 4, stride=2), :]
                lift_rows[16 * z + 4 * x : 16 * z + 4 * x + 4, 128 * c : 128 * c + 128] = piece
    stage[0:64] = dot(lift_rows[...], up[...])
    for pair in range(2):
        for x in range(4):
            even = stage[32 * pair + 4 * x : 32 * pair + 4 * x + 4, :]
            odd = stage[32 * pair + 16 + 4 * x : 32 * pair + 16 + 4 * x + 4, :]
            mid[pair + 1, x + 2, 2:6, :] = jnp.where(half, even, odd)
    for c in range(4):
        for z in range(2):
            for x in range(2):
                piece = mid[z + 1, 2 * x + c // 2 + 2, pl.ds(c % 2 + 2, 2, stride=2), :]
                lift_rows[4 * z + 2 * x : 4 * z + 2 * x + 2, 128 * c : 128 * c + 128] = piece
    stage[0:8] = dot(lift_rows[0:8], up[...])
    for x in range(2):
        even, odd = stage[2 * x : 2 * x + 2, :], stage[4 + 2 * x : 4 + 2 * x + 2, :]
        coarse[1, x + 2, 2:4, :] = jnp.where(half, even, odd)
    line = jnp.concatenate(
        [coarse[1, c // 2 + 2, c % 2 + 2 : c % 2 + 3, :] for c in range(4)], axis=1
    )
    tops_z[mz] = dot(jnp.broadcast_to(line, (8, 8 * Q)), up[...])

    pl.semaphore_wait(barrier, len(mates))
    multi = [
        Shift("gz", 1, 6, leaf.at[4, pl.ds(2, 8)], leaf.at[0, pl.ds(2, 8)]),
        Shift("gz", -1, 7, leaf.at[1, pl.ds(2, 8)], leaf.at[5, pl.ds(2, 8)]),
        Shift("gz", 1, 8, mid.at[2, pl.ds(2, 4)], mid.at[0, pl.ds(2, 4)]),
        Shift("gz", -1, 9, mid.at[1, pl.ds(2, 4)], mid.at[3, pl.ds(2, 4)]),
        Shift("gz", 1, 10, coarse.at[1, pl.ds(2, 2)], coarse.at[0, pl.ds(2, 2)]),
        Shift("gz", -1, 11, coarse.at[1, pl.ds(2, 2)], coarse.at[2, pl.ds(2, 2)]),
    ]
    index = 20
    for step in range(1, nz):
        multi.append(Spread("gz", step, index, tops_z.at[mz]))
        index += 1
    start(multi)
    shifts = [Shift("gz", 1 - 2 * s, s, pz_out.at[s], pz_in.at[s]) for s in range(2)]
    start(shifts)
    wait(multi)
    for pair in range(nz // 2):
        even, odd = tops_z[2 * pair, 0:1, :], tops_z[2 * pair + 1, 0:1, :]
        tops_y[my, pair : pair + 1, :] = jnp.where(half, even, odd)
    packed = []
    for ref, tiles, width in ((leaf, 6, 8), (mid, 4, 4), (coarse, 3, 2)):
        for tile in range(tiles):
            for x in range(width):
                packed.append((ref, tile, x + 2, width))
    for number, (ref, tile, x, width) in enumerate(packed):
        my_out[0, 2 * number : 2 * number + 2, :] = ref[tile, x, width : width + 2, :]
        my_out[1, 2 * number : 2 * number + 2, :] = ref[tile, x, 2:4, :]
    multi = [Shift("gy", 1 - 2 * s, 12 + s, my_out.at[s], my_in.at[s]) for s in range(2)]
    for step in range(1, ny):
        multi.append(Spread("gy", step, index, tops_y.at[my]))
        index += 1
    start(multi)

    wait(shifts)

    @pl.when(mz > 0)
    def _():
        for x in range(8):
            cells[x + 1, pl.ds(16, 8, stride=16), :] = pz_in[0, 8 * x : 8 * x + 8, :]

    @pl.when(mz < nz - 1)
    def _():
        for x in range(8):
            cells[x + 1, pl.ds(16 + 9, 8, stride=16), :] = pz_in[1, 8 * x : 8 * x + 8, :]

    inner = pl.ds(1, 8)
    shifts = [
        Shift("gy", 1, 2, cells.at[inner, pl.ds(128, 16)], cells.at[inner, pl.ds(0, 16)]),
        Shift("gy", -1, 3, cells.at[inner, pl.ds(16, 16)], cells.at[inner, pl.ds(144, 16)]),
    ]
    start(shifts)
    def put(target, pieces):
        turned = jnp.concatenate(pieces, axis=0).T
        sx, sy, sz = turned[0:32], turned[32:64], turned[64:96]
        target[0:128] = turned
        target[128:160] = (sx * sx + sy * sy) + sz * sz

    def column(x, y, oz):
        return cells[x, 16 * y + oz : 16 * y + oz + 8, :]

    def pair_turn(first, second, entry):
        for oz in range(3):
            put(planes.at[oz, entry], [column(x, y + 1, oz) for x in (first, second) for y in range(8)])

    def edge_turn(first, second, entry):
        for oz in range(3):
            pieces = []
            for x in (first, second):
                pieces += [column(x, 0, oz)] * 4 + [column(x, 9, oz)] * 4
            put(edges.at[oz, entry], pieces)

    def between(ref, low_entry, high_entry, entry):
        for oz in range(3):
            both = jnp.where(half, ref[oz, high_entry], ref[oz, low_entry])
            ref[oz, entry] = pltpu.roll(both, Q, 1)

    def pair_loop(k, carry):
        pair_turn(2 * k + 1, 2 * k + 2, 2 * k + 1)
        return carry

    def edge_loop(k, carry):
        edge_turn(2 * k + 1, 2 * k + 2, 2 * k + 1)
        return carry

    def between_loop(ref):
        def turn(k, carry):
            between(ref, 2 * k + 1, 2 * k + 3, 2 * k + 2)
            return carry

        lax.fori_loop(0, 3, turn, 0)

    group = lanes((8, 128)) // 32
    inside = lanes() % Q

    def spread_out(values, target, b):
        stage[...] = jnp.concatenate([values] * 4, axis=0).T
        for i in range(2):
            for block in range(2):
                result = None
                for z in range(4):
                    line = stage[pl.ds(64 * i + 4 * block + z, 8, stride=8), :]
                    result = line if z == 0 else jnp.where(group == z, line, result)
                target[2 * b + i, :, 128 * block : 128 * block + 128] = result

    def fill(target, entry, oz, oy):
        if oy < 0:
            target[...] = jnp.where(inside < 8, edges[oz, entry], pltpu.roll(planes[oz, entry], 8, 1))
        else:
            target[...] = jnp.where(
                inside >= 56, edges[oz, entry], pltpu.roll(planes[oz, entry], 120, 1)
            )

    def add(source, moves, oz, oy):
        sides = []
        dz = 2.0 * (oz - 1).astype(jnp.float32)
        for b, ox in moves:
            x = own_twice[b, 0:32] + 2.0 * ox
            y = own_twice[b, 32:64] + 2.0 * oy
            z = own_twice[b, 64:96] + dz
            sides.append((x, y, z, 0.25 * (x * x + y * y + z * z) + SOFTEN_SQUARED))

        def source_turn(p, values):
            sx, sy, sz = (source[pl.ds(32 * c + p, 1), :] for c in range(3))
            strength, length = source[pl.ds(96 + p, 1), :], source[pl.ds(128 + p, 1), :]
            result = []
            for (x, y, z, squared), value in zip(sides, values):
                distance = (squared + length) + (x * sx + y * sy + z * sz)
                result.append(value + lax.rsqrt(distance) * strength)
            return tuple(result)

        zero = jnp.zeros((32, 128), jnp.float32)
        values = lax.fori_loop(0, 32, source_turn, (zero,) * len(moves), unroll=32)
        for (b, ox), value in zip(moves, values):
            near_sum[b] += value

    def single_moves(k):
        return 2 * k + 1, [(k, 0.0)]

    def double_moves(k):
        return 2 * k + 2, [(k + 1, -1.0), (k, 1.0)]

    near_sum[...] = jnp.zeros_like(near_sum)
    lax.fori_loop(0, 4, pair_loop, 0)
    between_loop(planes)

    def straight_turn(number, carry):
        for oz in range(3):
            for entry, moves in (single_moves(number), double_moves(number)):
                add(planes.at[oz, entry], moves, jnp.int32(oz), 0)
        return carry

    lax.fori_loop(0, 1, straight_turn, 0)
    wait(multi)
    for y in range(ny):
        tops[mx, y * (nz // 2) : (y + 1) * (nz // 2), :] = tops_y[y, 0 : nz // 2, :]

    @pl.when(my > 0)
    def _():
        for number, (ref, tile, x, width) in enumerate(packed):
            ref[tile, x, 0:2, :] = my_in[0, 2 * number : 2 * number + 2, :]

    @pl.when(my < ny - 1)
    def _():
        for number, (ref, tile, x, width) in enumerate(packed):
            ref[tile, x, width + 2 : width + 4, :] = my_in[1, 2 * number : 2 * number + 2, :]

    multi = []
    for number, (ref, tiles, width) in enumerate(((leaf, 6, 8), (mid, 4, 4), (coarse, 3, 2))):
        every = pl.ds(0, tiles)
        left, right = ref.at[every, pl.ds(0, 2)], ref.at[every, pl.ds(width + 2, 2)]
        multi.append(Shift("gx", 1, 14 + 2 * number, ref.at[every, pl.ds(width, 2)], left))
        multi.append(Shift("gx", -1, 15 + 2 * number, ref.at[every, pl.ds(2, 2)], right))
    for step in range(1, nx):
        multi.append(Spread("gx", step, index, tops.at[mx]))
        index += 1
    start(multi)
    lax.fori_loop(1, 3, straight_turn, 0)
    for oz in range(3):
        add(planes.at[oz, 7], [(3, 0.0)], jnp.int32(oz), 0)

    wait(shifts)
    shifts = [
        Shift("gx", 1, 4, cells.at[8], cells.at[0]),
        Shift("gx", -1, 5, cells.at[1], cells.at[9]),
    ]
    start(shifts)
    lax.fori_loop(0, 4, edge_loop, 0)
    between_loop(edges)

    def shifted(parts, oz):
        slabs = iter((slab0, slab1, slab2, slab3))
        jobs = [(next(slabs), entry, moves, oy) for entry, moves in parts for oy in (-1, 1)]
        for slab, entry, moves, oy in jobs:
            fill(slab, entry, oz, oy)
        for slab, entry, moves, oy in jobs:
            add(slab, moves, oz, oy)

    def shifted_turn(number, carry):
        k = number // 3
        shifted([single_moves(k), double_moves(k)], number % 3)
        return carry

    lax.fori_loop(0, 6, shifted_turn, 0)
    wait(multi)
    for table in tables[3:]:
        table.wait()

    def split(values):
        first = values.astype(jnp.bfloat16)
        return first, (values - first.astype(jnp.float32)).astype(jnp.bfloat16)

    def wide_turn(ux, carry):
        for uy in range(8):
            for tile in range(6):
                for gx in range(2):
                    piece = leaf[tile, ux + 4 * gx, pl.ds(uy, 2, stride=4), :]
                    gather[uy, 4 * tile + 2 * gx : 4 * tile + 2 * gx + 2, :] = piece
        for uy in range(8):
            for t in range(3):
                first, second = split(gather[uy, 4 * t : 4 * t + 16, :])
                wide[0, ux, uy, :, 128 * t : 128 * t + 128] = first
                wide[1, ux, uy, :, 128 * t : 128 * t + 128] = second
        return carry

    lax.fori_loop(0, 8, wide_turn, 0)

    def narrow_turn(sx, carry):
        for sy in range(6):
            for tile in range(4):
                for gx in range(2):
                    piece = mid[tile, sx + 2 * gx, pl.ds(sy, 2, stride=2), :]
                    gather_mid[sy, 4 * tile + 2 * gx : 4 * tile + 2 * gx + 2, :] = piece
        for sy in range(6):
            for t in range(3):
                last = jnp.broadcast_to(coarse[t, sx, sy : sy + 1, :], (8, 128))
                both = jnp.concatenate([gather_mid[sy, 4 * t : 4 * t + 8, :], last], axis=0)
                first, second = split(both)
                narrow[0, sx, sy, :, 128 * t : 128 * t + 128] = first
                narrow[1, sx, sy, :, 128 * t : 128 * t + 128] = second
        return carry

    lax.fori_loop(0, 6, narrow_turn, 0)
    total[...] = jnp.zeros_like(total)

    def list_part(number):
        sx = number // 3
        lefts = []
        for k in range(2):
            sy = 2 * (number % 3) + k
            columns = []
            for h in range(2):
                columns += [wide[h, sx + 2 * (c // 2), sy + 2 * (c % 2)] for c in range(4)]
                columns.append(narrow[h, sx, sy])
            lefts.append(jnp.concatenate(columns, axis=0))
        left = jnp.concatenate(lefts, axis=1)
        for cx in range(2):

            def right(table):
                lines = []
                for k in range(2):
                    sy = 2 * (number % 3) + k
                    pieces = [table[sx + 1 - cx, sy + 1 - cy] for cy in range(2)]
                    lines.append(jnp.concatenate(pieces, axis=1))
                return jnp.concatenate(lines, axis=0)

            first = jnp.dot(left, right(high), preferred_element_type=jnp.float32)
            second = jnp.dot(left[:80], right(low), preferred_element_type=jnp.float32)
            total[:, 256 * cx : 256 * cx + 256] += first[:80] + first[80:] + second

    def mixed_turn(number, carry):
        list_part(2 * number)
        list_part(2 * number + 1)
        return shifted_turn(number + 6, carry)

    lax.fori_loop(0, 3, mixed_turn, 0)

    def last_turn(oz, carry):
        list_part(2 * oz + 6)
        list_part(2 * oz + 7)
        shifted([single_moves(3)], oz)
        return carry

    lax.fori_loop(0, 3, last_turn, 0)

    wait(shifts)
    for turn, ref in ((pair_turn, planes), (edge_turn, edges)):
        turn(9, 0, 9)
        between(ref, 9, 1, 0)
        between(ref, 7, 9, 8)

    def outer_turn(oz, carry):
        for k, part in enumerate(((0, [(0, -1.0)]), (8, [(3, 1.0)]))):
            list_part(2 * oz + 12 + k)
            entry, moves = part
            add(planes.at[oz, entry], moves, oz, 0)
            shifted([part], oz)
        return carry

    lax.fori_loop(0, 3, outer_turn, 0)
    for b in range(4):
        spread_out(near_sum[b], near_out, b)

    def far_turn(number, value):
        sx = number // (ny * (nz // 2))
        sy = number // (nz // 2) % ny
        sz = 2 * (number % (nz // 2))
        row = tops[sx, pl.ds(number % (ny * (nz // 2)), 1), :]
        dx = (mx - sx).astype(jnp.float32)
        dy = (my - sy).astype(jnp.float32)
        dz = (mz - sz).astype(jnp.float32) - jnp.where(half, 0.0, 1.0)
        first, second, third = base[0] + dx, base[1] + dy, base[2] + dz
        squared = first * first + second * second + third * third
        reach = jnp.maximum(jnp.maximum(jnp.abs(dx), jnp.abs(dy)), jnp.abs(dz))
        weight = jnp.where(reach >= 2.0, row * INV_FOUR_PI, 0.0)
        kernel = jnp.where(reach >= 2.0, lax.rsqrt(squared), 0.0)
        return value + kernel * weight

    zero = jnp.zeros((Q, 128), jnp.float32)
    checks = lax.fori_loop(0, nx * ny * (nz // 2), far_turn, zero, unroll=8)
    top_local = jnp.sum(dot(checks.T, fit[...]), axis=0, keepdims=True)

    fitted = jnp.concatenate(
        [dot(total[:, 128 * pair : 128 * pair + 128], pair_fit[...]) for pair in range(4)], axis=1
    )
    line = fitted[72:80] + dot(jnp.broadcast_to(top_local, (8, Q)), down[...])
    order = [2 * c + z for z in range(2) for c in range(4)]
    boxes = jnp.concatenate([line[0:1, Q * c : Q * c + Q] for c in order], axis=0)
    boxes = fitted[64:72] + dot(boxes, down[...])
    for c in range(4):
        for z in range(4):
            column = Q * (2 * c + z % 2)
            stage[16 * c + 4 * z : 16 * c + 4 * z + 4, 0:Q] = boxes[
                4 * (z // 2) : 4 * (z // 2) + 4, column : column + Q
            ]
    lines = fitted[0:64] + dot(stage[0:64, 0:Q], down[...])
    for h in range(4):
        local[h] = lines[:, 128 * h : 128 * h + 128]

    even = lanes() % 2 == 0
    slabs = (slab0, slab1, slab2, slab3)
    for b in range(4):
        for h in range(4):
            for cy in range(2):
                for gy in range(2):
                    start_row = 16 * (2 * (b % 2) + cy) + 2 * (b // 2) + gy
                    piece = local[h, pl.ds(start_row, 4, stride=4), :]
                    target = 64 * (h // 2) + 8 * (2 * (cy + 2 * gy) + h % 2)
                    stage[pl.ds(target, 4, stride=2), :] = piece
                    stage[pl.ds(target + 1, 4, stride=2), :] = piece
        turned = stage[...].T
        slabs[b][0:Q] = jnp.where(even, turned[0:Q], turned[Q : 2 * Q])

    for pair in range(2):
        sides = []
        for b in (2 * pair, 2 * pair + 1):
            x, y, z = own_twice[b, 0:32], own_twice[b, 32:64], own_twice[b, 64:96]
            sides.append((x, y, z, 0.25 * (x * x + y * y + z * z) + OUTER * OUTER, slabs[b]))

        def point_turn(k, values):
            px, py, pz = (spread[c, pl.ds(k, 1), :] for c in range(3))
            result = []
            for (x, y, z, squared, density), value in zip(sides, values):
                distance = squared + (x * px + y * py + z * pz)
                result.append(value + lax.rsqrt(distance) * density[pl.ds(k, 1), :])
            return tuple(result)

        first = (near_sum[2 * pair], near_sum[2 * pair + 1])
        values = lax.fori_loop(0, Q, point_turn, first, unroll=32)
        for b, value in zip((2 * pair, 2 * pair + 1), values):
            spread_out(value, potential, b)


def per_device(particles, counts):
    spread, fit_twice, up, base, fit, pair_fit, down, high, low = constant_tables()
    sizes = tuple(lax.axis_size(axis) for axis in AXES)
    nx, ny, nz = sizes
    copies = 20 + sum(sizes) - 3
    vmem = pl.BlockSpec(memory_space=pltpu.VMEM)
    remote = pl.BlockSpec(memory_space=pl.ANY)
    single = jnp.float32

    def array(*shape):
        return pltpu.VMEM(shape, single)

    outputs = pl.pallas_call(
        functools.partial(fused_kernel, sizes),
        out_shape=(jax.ShapeDtypeStruct((8, 8, 256), single),) * 2,
        in_specs=[vmem] * 2 + [remote] * 9,
        out_specs=(vmem, vmem),
        scratch_shapes=[
            array(*spread.shape),
            array(*fit_twice.shape),
            array(*up.shape),
            array(*base.shape),
            array(*fit.shape),
            array(*pair_fit.shape),
            array(*down.shape),
            array(10, 160, 128),
            array(3, 10, 160, 128),
            array(3, 10, 160, 128),
            array(4, 128, 128),
            array(4, 96, 128),
            array(160, 128),
            array(160, 128),
            array(160, 128),
            array(160, 128),
            array(160, 128),
            array(6, 12, 12, 128),
            array(4, 8, 8, 128),
            array(3, 6, 6, 128),
            array(nz, 8, 128),
            array(ny, -(-nz // 16) * 8, 128),
            array(nx, -(-ny * nz // 16) * 8, 128),
            array(128, 128),
            array(64, 512),
            array(2, 64, 128),
            array(2, 64, 128),
            array(2, 144, 128),
            array(2, 144, 128),
            array(8, 24, 128),
            array(6, 16, 128),
            pltpu.VMEM((2, 8, 8, 16, 384), jnp.bfloat16),
            pltpu.VMEM((2, 6, 6, 16, 384), jnp.bfloat16),
            array(80, 512),
            array(4, 32, 128),
            array(4, 64, 128),
            pltpu.VMEM(high.shape, jnp.bfloat16),
            pltpu.VMEM(low.shape, jnp.bfloat16),
            pltpu.SemaphoreType.DMA((copies,)),
            pltpu.SemaphoreType.DMA((copies,)),
            pltpu.SemaphoreType.DMA((9,)),
        ],
        compiler_params=pltpu.CompilerParams(
            collective_id=0, has_side_effects=True, vmem_limit_bytes=56 << 20
        ),
        cost_estimate=pl.CostEstimate(flops=8 << 30, bytes_accessed=12 << 20, transcendentals=0),
    )(particles, counts, spread, fit_twice, up, base, fit, pair_fit, down, high, low)
    return tuple(INV_FOUR_PI * output for output in outputs)


def solution(mesh):
    placed = (P("gx", "gy", "gz", None), P("gx", "gy", "gz"))
    return jax.shard_map(
        per_device,
        mesh=mesh,
        in_specs=placed,
        out_specs=(P("gx", "gy", "gz"), P("gx", "gy", "gz")),
        check_vma=False,
    )
```
